128 devices in a mesh: seq: 32 (over y, z, core), ch: 4 (over x).
Axes of the slice: x: 4, y: 4, z: 4, core: 2. Of those that a mesh axis runs over, the one named last changes fastest.
Arguments:
- query_proj: bfloat16 [8192, 8192], P('seq', 'ch'), may hold values from -6 to 6
- key_proj: bfloat16 [8192, 8192], P('seq', 'ch'), may hold values from -6 to 6
- value_proj: bfloat16 [8192, 8192], P('seq', 'ch'), may hold values from -6 to 6
- decay_rate: float32 [16, 8192], P(None, 'ch'), may hold values from 2.4414062e-06 to 0.033
- pole_angle: float32 [16, 8192], P(None, 'ch'), may hold values from -3.140625 to 3.140625
- residue_real: float32 [16, 8192], P(None, 'ch'), may hold values from -6 to 6
- residue_imag: float32 [16, 8192], P(None, 'ch'), may hold values from -6 to 6
- skip_gain: float32 [8192], P('ch'), may hold values from -6 to 6
- norm_gain: float32 [8192], P('ch'), may hold values from 0.5 to 1.5
Outputs:
- layer_out: bfloat16 [8192, 8192], P('seq', 'ch')
The draws below stay inside these ranges and needn't reach their ends.
All inputs are finite; a program needn't handle non-finite values.
Results may differ from the reference program's by a relative error of at most 0.0017.
Values sent between devices are 32-bit elements; how exact they have to be, the bound alone decides.
A program may use at most 64 MiB of HBM per device.

```python
import math
import jax
import jax.numpy as jnp
from jax import lax

D = 8192
MODES = 16
TOKENS = 8192


def shard_levels(own_key, dims, pieces, low, high):
    def one(position, parts):
        steps = jax.random.uniform(jax.random.fold_in(jax.random.fold_in(own_key, 6), position), (parts,), jnp.float32, low / len(pieces), high / len(pieces))
        return jnp.repeat(jnp.exp(steps), dims[position] // parts).reshape((-1,) + (1,) * (len(dims) - position - 1))

    gain = one(*pieces[0])
    for cut in pieces[1:]:
        gain = gain * one(*cut)
    return gain


def normal_values(stream_key, shape, width, reach, split=(), held_as=jnp.bfloat16):
    array = jax.random.normal(stream_key, shape, jnp.float32) * width
    if len(split) > 0:
        array = shard_levels(stream_key, shape, split, -0.22, 0.18) * array
    return jnp.clip(array, min=-reach, max=reach).astype(held_as)


def setup_inputs(seed: int = 0) -> dict:
    key_list = jax.random.split(jax.random.key(seed), 10)
    return {
        "query_proj": normal_values(key_list[0], (TOKENS, D), 1.0, 6.0, ((0, 32), (1, 4))),
        "key_proj": normal_values(key_list[1], (TOKENS, D), 1.0, 6.0, ((0, 32), (1, 4))),
        "value_proj": normal_values(key_list[2], (TOKENS, D), 1.0, 6.0, ((0, 32), (1, 4))),
        "decay_rate": jnp.clip(jnp.exp(math.log(0.033) - 9.5116887 * jax.random.uniform(key_list[3], (MODES, D), jnp.float32) ** shard_levels(key_list[3], (MODES, D), ((1, 4),), -0.2, 0.2)), 2.441406195430318e-06, 0.033),
        "pole_angle": jnp.clip(jax.random.uniform(key_list[4], (MODES, D), jnp.float32, -3.140625, 3.140625), -3.140625, 3.140625),
        "residue_real": normal_values(key_list[5], (MODES, D), 1.0, 6.0, ((1, 4),), jnp.float32),
        "residue_imag": normal_values(key_list[6], (MODES, D), 1.0, 6.0, ((1, 4),), jnp.float32),
        "skip_gain": normal_values(key_list[7], (D,), 1.0, 6.0, ((0, 4),), jnp.float32),
        "norm_gain": jnp.clip(1.0 + 0.1 * jax.random.normal(key_list[8], (D,), jnp.float32), 0.5, 1.5),
    }


def powers(decay_rate, pole_angle, count):
    magnitude = jnp.exp(-count * decay_rate)
    return (magnitude * jnp.cos(count * pole_angle), magnitude * jnp.sin(count * pole_angle))

def reference(query_proj, key_proj, value_proj, decay_rate, pole_angle, residue_real, residue_imag, skip_gain, norm_gain):
    highest = lax.Precision.HIGHEST
    mixed = key_proj.astype(jnp.float32) * value_proj.astype(jnp.float32)
    block_len = 64
    offsets = jnp.arange(block_len).astype(jnp.float32)[:, None, None]
    weight = jnp.sqrt(decay_rate)
    base_re, base_im = powers(decay_rate, pole_angle, offsets)
    taps = lax.optimization_barrier(jnp.sum(weight * (residue_real * base_re - residue_imag * base_im), axis=1))
    lag = jnp.arange(block_len)[:, None] - jnp.arange(block_len)[None, :]
    toeplitz = jnp.where((lag >= 0)[:, :, None], taps[jnp.clip(lag, 0, block_len - 1)], 0.0)
    next_re, next_im = powers(decay_rate, pole_angle, offsets + 1.0)
    out_re = weight * (residue_real * next_re - residue_imag * next_im)
    out_im = weight * (residue_real * next_im + residue_imag * next_re)
    in_re, in_im = powers(decay_rate, pole_angle, block_len - 1.0 - offsets)
    step_re, step_im = powers(decay_rate, pole_angle, jnp.float32(block_len))
    blocks = mixed.reshape(mixed.shape[0] // block_len, block_len, mixed.shape[1])

    def advance(carry, block):
        state_re, state_im = carry
        near = jnp.einsum('tsc,sc->tc', toeplitz, block, precision=highest)
        far = jnp.einsum('jmc,mc->jc', out_re, state_re, precision=highest) - jnp.einsum('jmc,mc->jc', out_im, state_im, precision=highest)
        enter_re = jnp.einsum('jmc,jc->mc', in_re, block, precision=highest)
        enter_im = jnp.einsum('jmc,jc->mc', in_im, block, precision=highest)
        new_re = step_re * state_re - step_im * state_im + enter_re
        new_im = step_re * state_im + step_im * state_re + enter_im
        return ((new_re, new_im), near + far)
    zeros = jnp.zeros_like(decay_rate)
    final_state, outputs = lax.scan(advance, (zeros, zeros), blocks)
    conv = outputs.reshape(mixed.shape)
    gated = query_proj.astype(jnp.float32) * (conv + skip_gain * mixed)
    power = lax.optimization_barrier(jnp.mean(gated * gated, axis=1, keepdims=True))
    return (gated * norm_gain * lax.rsqrt(power + 1e-05)).astype(jnp.bfloat16)
```

```python
import functools
import math

import jax
import jax.numpy as jnp
from jax import lax
from jax.experimental import pallas as pl
from jax.experimental.pallas import tpu as pltpu
from jax.sharding import PartitionSpec as P

F32 = jnp.float32
MODES = 16
CHUNK = 16
LANES = 128
HALF = 8
EPS = 1e-05


def aligned(value, step):
    return pl.multiple_of(value, step)


def cmul(a, b):
    return a[0] * b[0] - a[1] * b[1], a[0] * b[1] + a[1] * b[0]


def csquare(a):
    cross = a[0] * a[1]
    return a[0] * a[0] - a[1] * a[1], cross + cross


def cadd(a, b):
    return a[0] + b[0], a[1] + b[1]


def sin_cos(angle):
    z = angle * 0.5
    w = z * z
    s = jnp.full_like(w, 1.0 / math.factorial(13))
    for n in (11, 9, 7, 5, 3, 1):
        s = s * w + ((-1.0) ** ((n - 1) // 2)) / math.factorial(n)
    s = s * z
    c = jnp.full_like(w, 1.0 / math.factorial(12))
    for n in (10, 8, 6, 4, 2, 0):
        c = c * w + ((-1.0) ** (n // 2)) / math.factorial(n)
    sc = s * c
    return sc + sc, 1.0 - 2.0 * (s * s)


def whole_power(decay, angle, count):
    v = angle * float(count)
    turns = jnp.floor(v * (0.5 / math.pi) + 0.5)
    first = 6.28125
    second = round((2.0 * math.pi - first) * 2.0**23) / 2.0**23
    third = 2.0 * math.pi - first - second
    rest = ((v - turns * first) - turns * second) - turns * third
    s, c = sin_cos(rest)
    magnitude = jnp.exp(decay * -float(count))
    return magnitude * c, magnitude * s


def kernel(
    n_seq,
    n_ch,
    q_hbm,
    k_hbm,
    v_hbm,
    decay_ref,
    angle_ref,
    res_re_ref,
    res_im_ref,
    skip_ref,
    gain_ref,
    out_ref,
    q_buf,
    k_buf,
    v_buf,
    xs,
    ys,
    par,
    taps,
    zs,
    table,
    qpow,
    e_stage,
    e_all,
    s_out,
    s_all,
    p_all,
    in_sems,
    e_send,
    e_recv,
    s_send,
    s_recv,
    p_send,
    p_recv,
    own_sems,
):
    me = lax.axis_index("seq")
    my_ch = lax.axis_index("ch")
    tokens = q_buf.shape[0]
    rows = q_buf.shape[1] // LANES
    chunks = tokens // CHUNK
    halves = rows // HALF
    slices = MODES * halves

    loads = [
        pltpu.make_async_copy(k_hbm, k_buf, in_sems.at[0]),
        pltpu.make_async_copy(v_hbm, v_buf, in_sems.at[1]),
        pltpu.make_async_copy(q_hbm, q_buf, in_sems.at[2]),
    ]
    for load in loads:
        load.start()

    barrier = pltpu.get_barrier_semaphore()

    @pl.loop(1, n_seq)
    def _(step):
        pl.semaphore_signal(barrier, inc=1, device_id={"seq": lax.rem(me + step, n_seq)}, device_id_type=pl.DeviceIdType.MESH)

    @pl.loop(1, n_ch)
    def _(step):
        pl.semaphore_signal(barrier, inc=1, device_id={"ch": lax.rem(my_ch + step, n_ch)}, device_id_type=pl.DeviceIdType.MESH)

    @pl.loop(0, rows)
    def _(r):
        lanes = pl.ds(aligned(r * LANES, LANES), LANES)
        place = pl.ds(r, MODES, stride=rows)
        decay = decay_ref[:, lanes]
        angle = angle_ref[:, lanes]
        s, c = sin_cos(angle)
        magnitude = jnp.exp(-decay)
        weight = jnp.sqrt(decay)
        par[0, place, :] = magnitude * c
        par[1, place, :] = magnitude * s
        par[2, place, :] = weight * res_re_ref[:, lanes]
        par[3, place, :] = weight * res_im_ref[:, lanes]
        par[4, place, :] = decay
        par[5, place, :] = angle

    loads[0].wait()
    loads[1].wait()

    @pl.loop(0, tokens // 16)
    def _(g):
        toks = pl.ds(aligned(g * 16, 16), 16)
        for r in range(rows):
            lanes = pl.ds(r * LANES, LANES)
            xs[pl.ds(g * (16 * rows) + r, 16, stride=rows), :] = k_buf[toks, lanes].astype(F32) * v_buf[toks, lanes].astype(F32)

    zero = jnp.zeros((HALF, LANES), F32)
    for h in range(halves):
        taps[0, h] = skip_ref[pl.ds(h * HALF, HALF), :]
        for n in range(1, CHUNK):
            taps[n, h] = zero

    pl.semaphore_wait(barrier, n_seq - 1 + n_ch - 1)

    def own_copy_e(i):
        return pltpu.make_async_copy(e_stage.at[i], e_all.at[me], own_sems.at[0])

    def remote_e(i):
        return pltpu.make_async_remote_copy(
            src_ref=e_stage.at[i],
            dst_ref=e_all.at[me],
            send_sem=e_send.at[i],
            recv_sem=e_recv.at[me],
            device_id={"seq": i},
            device_id_type=pl.DeviceIdType.MESH,
        )

    @pl.loop(0, slices)
    def _(i):
        m = i // halves
        h = lax.rem(i, halves)
        row = aligned(m * rows + h * HALF, HALF)
        here = pl.ds(row, HALF)
        pole = (par[0, here, :], par[1, here, :])
        w = (par[2, here, :], par[3, here, :])
        z = [None] * chunks
        for n in range(CHUNK):
            taps[n, h] += w[0]
            for j in range(chunks):
                x = xs[pl.ds(aligned((j * CHUNK + CHUNK - 1 - n) * rows + h * HALF, HALF), HALF), :]
                term = (w[0] * x, w[1] * x)
                z[j] = term if n == 0 else cadd(z[j], term)
            if n < CHUNK - 1:
                w = cmul(w, pole)
        power = pole
        for _ in range(4):
            power = csquare(power)
        for j in range(chunks):
            zs[i, j, 0] = z[j][0]
            zs[i, j, 1] = z[j][1]
        level = 0
        while len(z) > 1:
            qpow[i, level, 0] = power[0]
            qpow[i, level, 1] = power[1]
            z = [cadd(cmul(z[2 * j], power), z[2 * j + 1]) for j in range(len(z) // 2)]
            level += 1
            if len(z) > 1:
                power = csquare(power)
        e_stage[i, 0] = z[0][0]
        e_stage[i, 1] = z[0][1]

        @pl.when(i != me)
        def _():
            remote_e(i).start()

        @pl.when(i == me)
        def _():
            own_copy_e(i).start()

    for h in range(halves):

        @pl.loop(0, chunks)
        def _(j):
            tap = [taps[n, h] for n in range(CHUNK)]
            x = [xs[pl.ds(aligned((j * CHUNK + s) * rows + h * HALF, HALF), HALF), :] for s in range(CHUNK)]
            for t in range(CHUNK):
                total = tap[t] * x[0]
                for s in range(1, t + 1):
                    total = total + tap[t - s] * x[s]
                ys[pl.ds(aligned((j * CHUNK + t) * rows + h * HALF, HALF), HALF), :] = total

    group = 4

    @pl.loop(0, slices // group)
    def _(b):
        ids = [b * group + u for u in range(group)]
        step = [(qpow[i, 0, 0], qpow[i, 0, 1]) for i in ids]
        states = [(zs[i, 0, 0], zs[i, 0, 1]) for i in ids]
        poles = []
        for i in ids:
            here = pl.ds(aligned((i // halves) * rows + lax.rem(i, halves) * HALF, HALF), HALF)
            poles.append((par[0, here, :], par[1, here, :]))
        powers = list(poles)
        for j in range(1, chunks):
            for u, i in enumerate(ids):
                if j < chunks - 1:
                    following = cadd(cmul(states[u], step[u]), (zs[i, j, 0], zs[i, j, 1]))
                zs[i, j, 0] = states[u][0]
                zs[i, j, 1] = states[u][1]
                if j < chunks - 1:
                    states[u] = following
        for t in range(CHUNK):
            for u, i in enumerate(ids):
                table[i, t, 0] = powers[u][0]
                table[i, t, 1] = powers[u][1]
                if t < CHUNK - 1:
                    powers[u] = cmul(powers[u], poles[u])

    mine = pl.ds(aligned((me // halves) * rows + lax.rem(me, halves) * HALF, HALF), HALF)
    jump = whole_power(par[4, mine, :], par[5, mine, :], tokens)

    own_copy_e(me).wait()

    @pl.loop(1, n_seq)
    def _(step):
        src = lax.rem(me + step, n_seq)
        pltpu.make_async_remote_copy(
            src_ref=e_stage.at[0],
            dst_ref=e_all.at[src],
            send_sem=e_send.at[0],
            recv_sem=e_recv.at[src],
            device_id={"seq": src},
            device_id_type=pl.DeviceIdType.MESH,
        ).wait_recv()

    def scan(d, state):
        s_out[d, 0] = state[0]
        s_out[d, 1] = state[1]
        return cadd(cmul(state, jump), (e_all[d, 0], e_all[d, 1]))

    lax.fori_loop(0, n_seq, scan, (zero, zero))

    def own_copy_s():
        return pltpu.make_async_copy(s_out.at[me], s_all.at[me], own_sems.at[1])

    def remote_s(dst):
        return pltpu.make_async_remote_copy(
            src_ref=s_out.at[dst],
            dst_ref=s_all.at[me],
            send_sem=s_send.at[dst],
            recv_sem=s_recv.at[me],
            device_id={"seq": dst},
            device_id_type=pl.DeviceIdType.MESH,
        )

    own_copy_s().start()

    @pl.loop(1, n_seq)
    def _(step):
        remote_s(lax.rem(me + step, n_seq)).start()

    own_copy_s().wait()

    def wait_state(i):
        @pl.when(i != me)
        def _():
            pltpu.make_async_remote_copy(
                src_ref=s_out.at[0],
                dst_ref=s_all.at[i],
                send_sem=s_send.at[0],
                recv_sem=s_recv.at[i],
                device_id={"seq": i},
                device_id_type=pl.DeviceIdType.MESH,
            ).wait_recv()

    pair = 2
    block = chunks // 2

    @pl.loop(0, slices // pair)
    def _(b):
        h = lax.rem(b, halves)
        first = (b // halves) * (pair * halves) + h
        ids = [first + u * halves for u in range(pair)]
        for i in ids:
            wait_state(i)
        starts = []
        for i in ids:
            d = [(s_all[i, 0], s_all[i, 1])]
            for level in range(3):
                power = (qpow[i, level, 0], qpow[i, level, 1])
                d = d + [cmul(a, power) for a in d]
            starts.append(d)
        for part in range(2):
            states = []
            for u, i in enumerate(ids):
                if part == 1:
                    power = (qpow[i, 3, 0], qpow[i, 3, 1])
                    starts[u] = [cmul(a, power) for a in starts[u]]
                states.append(
                    [
                        starts[u][j]
                        if part == 0 and j == 0
                        else cadd(starts[u][j], (zs[i, part * block + j, 0], zs[i, part * block + j, 1]))
                        for j in range(block)
                    ]
                )
            for t in range(CHUNK):
                power = [(table[i, t, 0], table[i, t, 1]) for i in ids]
                for j in range(block):
                    at = pl.ds(aligned(((part * block + j) * CHUNK + t) * rows + h * HALF, HALF), HALF)
                    total = ys[at, :]
                    for u in range(pair):
                        total = total + (power[u][0] * states[u][j][0] - power[u][1] * states[u][j][1])
                    ys[at, :] = total

    loads[2].wait()
    lane = lax.broadcasted_iota(jnp.int32, (16, LANES), 1)

    def gate(g, power):
        toks = pl.ds(aligned(g * 16, 16), 16)
        squares = jnp.zeros((16, LANES), F32)
        for r in range(rows):
            lanes = pl.ds(r * LANES, LANES)
            at = pl.ds(g * (16 * rows) + r, 16, stride=rows)
            gated = q_buf[toks, lanes].astype(F32) * ys[at, :]
            xs[pl.ds(aligned((g * rows + r) * 16, 16), 16), :] = gated
            squares = squares + gated * gated
        return jnp.where(lane == g, jnp.sum(squares, axis=1, keepdims=True), power)

    p_all[my_ch] = lax.fori_loop(0, tokens // 16, gate, jnp.zeros((16, LANES), F32))

    def remote_p(dst, src):
        return pltpu.make_async_remote_copy(
            src_ref=p_all.at[src],
            dst_ref=p_all.at[src],
            send_sem=p_send.at[dst],
            recv_sem=p_recv.at[src],
            device_id={"ch": dst},
            device_id_type=pl.DeviceIdType.MESH,
        )

    for step in range(1, n_ch):
        remote_p(lax.rem(my_ch + step, n_ch), my_ch).start()
    for step in range(1, n_ch):
        other = lax.rem(my_ch + step, n_ch)
        remote_p(other, other).wait_recv()
    total = p_all[0]
    for c in range(1, n_ch):
        total = total + p_all[c]
    p_all[n_ch] = lax.rsqrt(total * (1.0 / (rows * LANES * n_ch)) + EPS)

    @pl.loop(0, tokens // 16)
    def _(g):
        toks = pl.ds(aligned(g * 16, 16), 16)
        scale = jnp.sum(jnp.where(lane == g, p_all[n_ch], 0.0), axis=1, keepdims=True)
        scale = jnp.broadcast_to(scale, (16, LANES))
        for r in range(rows):
            lanes = pl.ds(r * LANES, LANES)
            gated = xs[pl.ds(aligned((g * rows + r) * 16, 16), 16), :]
            out_ref[toks, lanes] = (gated * gain_ref[:, lanes] * scale).astype(out_ref.dtype)

    @pl.loop(0, slices)
    def _(i):
        @pl.when(i != me)
        def _():
            remote_e(i).wait_send()
            remote_s(i).wait_send()

    for step in range(1, n_ch):
        remote_p(lax.rem(my_ch + step, n_ch), my_ch).wait_send()


def per_device(n_seq, n_ch, query, key, value, decay, angle, res_re, res_im, skip, gain):
    tokens, width = query.shape
    rows = width // LANES
    halves = rows // HALF
    slices = MODES * halves
    chunks = tokens // CHUNK
    if slices != n_seq or rows != 16 or chunks != 16:
        raise ValueError("unsupported sizes")
    tile = (HALF, LANES)
    anywhere = pl.BlockSpec(memory_space=pl.ANY)
    vmem = pl.BlockSpec(memory_space=pltpu.VMEM)
    dma = pltpu.SemaphoreType.DMA
    return pl.pallas_call(
        functools.partial(kernel, n_seq, n_ch),
        out_shape=jax.ShapeDtypeStruct((tokens, width), jnp.bfloat16),
        in_specs=[anywhere] * 3 + [vmem] * 6,
        out_specs=vmem,
        scratch_shapes=[
            pltpu.VMEM((tokens, width), jnp.bfloat16),
            pltpu.VMEM((tokens, width), jnp.bfloat16),
            pltpu.VMEM((tokens, width), jnp.bfloat16),
            pltpu.VMEM((tokens * rows, LANES), F32),
            pltpu.VMEM((tokens * rows, LANES), F32),
            pltpu.VMEM((6, MODES * rows, LANES), F32),
            pltpu.VMEM((CHUNK, halves) + tile, F32),
            pltpu.VMEM((slices, chunks, 2) + tile, F32),
            pltpu.VMEM((slices, CHUNK, 2) + tile, F32),
            pltpu.VMEM((slices, 4, 2) + tile, F32),
            pltpu.VMEM((slices, 2) + tile, F32),
            pltpu.VMEM((n_seq, 2) + tile, F32),
            pltpu.VMEM((n_seq, 2) + tile, F32),
            pltpu.VMEM((slices, 2) + tile, F32),
            pltpu.VMEM((n_ch + 1, 16, LANES), F32),
            dma((3,)),
            dma((slices,)),
            dma((n_seq,)),
            dma((n_seq,)),
            dma((slices,)),
            dma((n_ch,)),
            dma((n_ch,)),
            dma((2,)),
        ],
        compiler_params=pltpu.CompilerParams(collective_id=0, has_side_effects=True),
    )(query, key, value, decay, angle, res_re, res_im, skip.reshape(rows, LANES), gain.reshape(1, width))


def solution(mesh):
    in_specs = (
        P("seq", "ch"),
        P("seq", "ch"),
        P("seq", "ch"),
        P(None, "ch"),
        P(None, "ch"),
        P(None, "ch"),
        P(None, "ch"),
        P("ch"),
        P("ch"),
    )
    return jax.shard_map(
        functools.partial(per_device, mesh.shape["seq"], mesh.shape["ch"]),
        mesh=mesh,
        in_specs=in_specs,
        out_specs=P("seq", "ch"),
        check_vma=False,
    )
```

```python
import functools
import math

import jax
import jax.numpy as jnp
from jax import lax
from jax.experimental import pallas as pl
from jax.experimental.pallas import tpu as pltpu
from jax.sharding import PartitionSpec as P

F32 = jnp.float32
MODES = 16
CHUNK = 16
LANES = 128
HALF = 8
EPS = 1e-05
ROW_LEN = 8
MESH_IDS = pl.DeviceIdType.MESH


def aligned(value, step):
    return pl.multiple_of(value, step)


def cmul(a, b):
    return a[0] * b[0] - a[1] * b[1], a[0] * b[1] + a[1] * b[0]


def csquare(a):
    cross = a[0] * a[1]
    return a[0] * a[0] - a[1] * a[1], cross + cross


def cadd(a, b):
    return a[0] + b[0], a[1] + b[1]


def sin_cos(angle):
    z = angle * 0.5
    w = z * z
    s = jnp.full_like(w, 1.0 / math.factorial(13))
    for n in (11, 9, 7, 5, 3, 1):
        s = s * w + ((-1.0) ** ((n - 1) // 2)) / math.factorial(n)
    s = s * z
    c = jnp.full_like(w, 1.0 / math.factorial(12))
    for n in (10, 8, 6, 4, 2, 0):
        c = c * w + ((-1.0) ** (n // 2)) / math.factorial(n)
    sc = s * c
    return sc + sc, 1.0 - 2.0 * (s * s)


def whole_power(decay, angle, count):
    v = angle * float(count)
    turns = jnp.floor(v * (0.5 / math.pi) + 0.5)
    first = 6.28125
    second = round((2.0 * math.pi - first) * 2.0**23) / 2.0**23
    third = 2.0 * math.pi - first - second
    rest = ((v - turns * first) - turns * second) - turns * third
    s, c = sin_cos(rest)
    magnitude = jnp.exp(decay * -float(count))
    return magnitude * c, magnitude * s


def exchange_kernel(
    n_seq,
    n_ch,
    row_len,
    q_hbm,
    k_hbm,
    v_hbm,
    decay_hbm,
    angle_hbm,
    res_re_hbm,
    res_im_hbm,
    skip_hbm,
    gated_ref,
    scale_ref,
    q_buf,
    k_buf,
    v_buf,
    raw,
    skip_buf,
    xs,
    ys,
    par,
    taps,
    zs,
    table,
    qpow,
    e_stage,
    e_row,
    t_out,
    t_all,
    s_out,
    s_all,
    p_all,
    raw_sems,
    kv_sems,
    q_sem,
    e_send,
    e_recv,
    t_send,
    t_recv,
    s_send,
    s_recv,
    p_send,
    p_recv,
):
    me = lax.axis_index("seq")
    my_ch = lax.axis_index("ch")
    my_row = me // row_len
    my_k = lax.rem(me, row_len)
    n_rows = n_seq // row_len
    tokens = q_buf.shape[0]
    rows = q_buf.shape[1] // LANES
    chunks = tokens // CHUNK
    halves = rows // HALF
    slices = MODES * halves
    groups = slices // row_len

    raw_loads = [
        pltpu.make_async_copy(src, raw.at[n], raw_sems.at[n])
        for n, src in enumerate((decay_hbm, angle_hbm, res_re_hbm, res_im_hbm))
    ]
    raw_loads.append(pltpu.make_async_copy(skip_hbm, skip_buf, raw_sems.at[4]))
    for load in raw_loads:
        load.start()
    parts = kv_sems.shape[1]
    kv_loads = []
    for n in range(parts):
        toks = pl.ds(n * (tokens // parts), tokens // parts)
        kv_loads.append(
            [
                pltpu.make_async_copy(k_hbm.at[toks], k_buf.at[toks], kv_sems.at[0, n]),
                pltpu.make_async_copy(v_hbm.at[toks], v_buf.at[toks], kv_sems.at[1, n]),
            ]
        )
        for load in kv_loads[-1]:
            load.start()
    q_load = pltpu.make_async_copy(q_hbm, q_buf, q_sem)
    q_load.start()

    def in_row(k):
        return {"seq": my_row * row_len + k}

    def other_k(step):
        return lax.rem(my_k + step, row_len)

    barrier = pltpu.get_barrier_semaphore()

    @pl.loop(1, row_len)
    def _(step):
        pl.semaphore_signal(barrier, inc=1, device_id=in_row(other_k(step)), device_id_type=MESH_IDS)

    @pl.loop(1, n_rows)
    def _(step):
        row = lax.rem(my_row + step, n_rows)
        pl.semaphore_signal(barrier, inc=1, device_id={"seq": row * row_len + my_k}, device_id_type=MESH_IDS)

    @pl.loop(1, n_ch)
    def _(step):
        pl.semaphore_signal(barrier, inc=1, device_id={"ch": lax.rem(my_ch + step, n_ch)}, device_id_type=MESH_IDS)

    for load in raw_loads:
        load.wait()

    @pl.loop(0, rows)
    def _(r):
        lanes = pl.ds(aligned(r * LANES, LANES), LANES)
        place = pl.ds(r, MODES, stride=rows)
        decay = raw[0, :, lanes]
        angle = raw[1, :, lanes]
        s, c = sin_cos(angle)
        magnitude = jnp.exp(-decay)
        weight = jnp.sqrt(decay)
        par[0, place, :] = magnitude * c
        par[1, place, :] = magnitude * s
        par[2, place, :] = weight * raw[2, :, lanes]
        par[3, place, :] = weight * raw[3, :, lanes]
        par[4, place, :] = decay
        par[5, place, :] = angle

    zero = jnp.zeros((HALF, LANES), F32)
    for h in range(halves):
        taps[0, h] = skip_buf[pl.ds(h * HALF, HALF), :]
        for n in range(1, CHUNK):
            taps[n, h] = zero

    @pl.when(me == 0)
    def _():
        @pl.loop(0, slices)
        def _(i):
            s_all[i, 0] = zero
            s_all[i, 1] = zero

    per_part = tokens // parts // 16
    for n in range(parts):
        for load in kv_loads[n]:
            load.wait()

        @pl.loop(n * per_part, (n + 1) * per_part)
        def _(g):
            toks = pl.ds(aligned(g * 16, 16), 16)
            for r in range(rows):
                lanes = pl.ds(r * LANES, LANES)
                xs[pl.ds(g * (16 * rows) + r, 16, stride=rows), :] = k_buf[toks, lanes].astype(F32) * v_buf[toks, lanes].astype(F32)

    def own_slice(g):
        i = g * row_len + my_k
        return pl.ds(aligned((i // halves) * rows + lax.rem(i, halves) * HALF, HALF), HALF)

    def enter(g):
        @pl.loop(g * row_len, (g + 1) * row_len)
        def _(i):
            m = i // halves
            h = lax.rem(i, halves)
            here = pl.ds(aligned(m * rows + h * HALF, HALF), HALF)
            pole = (par[0, here, :], par[1, here, :])
            w = (par[2, here, :], par[3, here, :])
            z = [None] * chunks
            for n in range(CHUNK):
                taps[n, h] += w[0]
                for j in range(chunks):
                    x = xs[pl.ds(aligned((j * CHUNK + CHUNK - 1 - n) * rows + h * HALF, HALF), HALF), :]
                    term = (w[0] * x, w[1] * x)
                    z[j] = term if n == 0 else cadd(z[j], term)
                if n < CHUNK - 1:
                    w = cmul(w, pole)
            power = pole
            for _ in range(4):
                power = csquare(power)
            for j in range(chunks):
                zs[i, j, 0] = z[j][0]
                zs[i, j, 1] = z[j][1]
            level = 0
            while len(z) > 1:
                qpow[i, level, 0] = power[0]
                qpow[i, level, 1] = power[1]
                z = [cadd(cmul(z[2 * j], power), z[2 * j + 1]) for j in range(len(z) // 2)]
                level += 1
                if len(z) > 1:
                    power = csquare(power)
            e_stage[i, 0] = z[0][0]
            e_stage[i, 1] = z[0][1]

        e_row[g, my_k] = e_stage[g * row_len + my_k]

    def remote_e(g, k):
        return pltpu.make_async_remote_copy(
            src_ref=e_stage.at[g * row_len + k],
            dst_ref=e_row.at[g, my_k],
            send_sem=e_send.at[g, k],
            recv_sem=e_recv.at[g, my_k],
            device_id=in_row(k),
            device_id_type=MESH_IDS,
        )

    def remote_t(g, row):
        return pltpu.make_async_remote_copy(
            src_ref=t_out.at[g],
            dst_ref=t_all.at[g, my_row],
            send_sem=t_send.at[g, row],
            recv_sem=t_recv.at[g, my_row],
            device_id={"seq": row * row_len + my_k},
            device_id_type=MESH_IDS,
        )

    def remote_s(g, k):
        return pltpu.make_async_remote_copy(
            src_ref=s_out.at[g, k],
            dst_ref=s_all.at[g * row_len + my_k],
            send_sem=s_send.at[g, k],
            recv_sem=s_recv.at[g, my_k],
            device_id=in_row(k),
            device_id_type=MESH_IDS,
        )

    def send_e(g):
        @pl.loop(1, row_len)
        def _(step):
            remote_e(g, other_k(step)).start()

    def send_t(g):
        @pl.loop(1, row_len)
        def _(step):
            k = other_k(step)
            pltpu.make_async_remote_copy(
                src_ref=e_stage.at[0],
                dst_ref=e_row.at[g, k],
                send_sem=e_send.at[g, k],
                recv_sem=e_recv.at[g, k],
                device_id=in_row(k),
                device_id_type=MESH_IDS,
            ).wait_recv()

        jump = whole_power(par[4, own_slice(g), :], par[5, own_slice(g), :], tokens)
        total = (e_row[g, 0, 0], e_row[g, 0, 1])
        for k in range(1, row_len):
            total = cadd(cmul(total, jump), (e_row[g, k, 0], e_row[g, k, 1]))
        t_out[g, 0] = total[0]
        t_out[g, 1] = total[1]

        @pl.loop(1, n_rows)
        def _(step):
            @pl.when(my_row + step < n_rows)
            def _():
                remote_t(g, my_row + step).start()

    def send_s(g):
        decay, angle = par[4, own_slice(g), :], par[5, own_slice(g), :]
        jump = whole_power(decay, angle, tokens)
        row_jump = whole_power(decay, angle, tokens * row_len)

        def add_row(row, state):
            pltpu.make_async_remote_copy(
                src_ref=t_out.at[g],
                dst_ref=t_all.at[g, row],
                send_sem=t_send.at[g, row],
                recv_sem=t_recv.at[g, row],
                device_id={"seq": row * row_len + my_k},
                device_id_type=MESH_IDS,
            ).wait_recv()
            return cadd(cmul(state, row_jump), (t_all[g, row, 0], t_all[g, row, 1]))

        state = lax.fori_loop(0, my_row, add_row, (zero, zero))
        for k in range(row_len):
            s_out[g, k, 0] = state[0]
            s_out[g, k, 1] = state[1]
            if k < row_len - 1:
                state = cadd(cmul(state, jump), (e_row[g, k, 0], e_row[g, k, 1]))
        s_all[g * row_len + my_k] = s_out[g, my_k]

        @pl.loop(1, row_len)
        def _(step):
            k = other_k(step)

            @pl.when(my_row + k > 0)
            def _():
                remote_s(g, k).start()

    def near(h):
        @pl.loop(0, chunks)
        def _(j):
            tap = [taps[n, h] for n in range(CHUNK)]
            x = [xs[pl.ds(aligned((j * CHUNK + s) * rows + h * HALF, HALF), HALF), :] for s in range(CHUNK)]
            for t in range(CHUNK):
                total = tap[t] * x[0]
                for s in range(1, t + 1):
                    total = total + tap[t - s] * x[s]
                ys[pl.ds(aligned((j * CHUNK + t) * rows + h * HALF, HALF), HALF), :] = total

    def prepare(g):
        unit = 4

        @pl.loop(0, row_len // unit)
        def _(b):
            ids = [g * row_len + b * unit + u for u in range(unit)]
            step = [(qpow[i, 0, 0], qpow[i, 0, 1]) for i in ids]
            states = [(zs[i, 0, 0], zs[i, 0, 1]) for i in ids]
            poles = []
            for i in ids:
                here = pl.ds(aligned((i // halves) * rows + lax.rem(i, halves) * HALF, HALF), HALF)
                poles.append((par[0, here, :], par[1, here, :]))
            powers = list(poles)
            for j in range(1, chunks):
                for u, i in enumerate(ids):
                    if j < chunks - 1:
                        following = cadd(cmul(states[u], step[u]), (zs[i, j, 0], zs[i, j, 1]))
                    zs[i, j, 0] = states[u][0]
                    zs[i, j, 1] = states[u][1]
                    if j < chunks - 1:
                        states[u] = following
            for t in range(CHUNK):
                for u, i in enumerate(ids):
                    table[i, t, 0] = powers[u][0]
                    table[i, t, 1] = powers[u][1]
                    if t < CHUNK - 1:
                        powers[u] = cmul(powers[u], poles[u])

    pair = 2
    block = chunks // 2

    def far(g):
        @pl.when(me > 0)
        def _():
            @pl.loop(1, row_len)
            def _(step):
                k = other_k(step)
                pltpu.make_async_remote_copy(
                    src_ref=s_out.at[0, 0],
                    dst_ref=s_all.at[g * row_len + k],
                    send_sem=s_send.at[g, k],
                    recv_sem=s_recv.at[g, k],
                    device_id=in_row(k),
                    device_id_type=MESH_IDS,
                ).wait_recv()

        @pl.loop(0, row_len // pair)
        def _(b):
            h = lax.rem(b, halves)
            first = g * row_len + (b // halves) * (pair * halves) + h
            ids = [first + u * halves for u in range(pair)]
            starts = []
            for i in ids:
                d = [(s_all[i, 0], s_all[i, 1])]
                for level in range(3):
                    power = (qpow[i, level, 0], qpow[i, level, 1])
                    d = d + [cmul(a, power) for a in d]
                starts.append(d)
            for part in range(2):
                states = []
                for u, i in enumerate(ids):
                    if part == 1:
                        power = (qpow[i, 3, 0], qpow[i, 3, 1])
                        starts[u] = [cmul(a, power) for a in starts[u]]
                    states.append(
                        [
                            starts[u][j]
                            if part == 0 and j == 0
                            else cadd(starts[u][j], (zs[i, part * block + j, 0], zs[i, part * block + j, 1]))
                            for j in range(block)
                        ]
                    )
                for t in range(CHUNK):
                    power = [(table[i, t, 0], table[i, t, 1]) for i in ids]
                    for j in range(block):
                        at = pl.ds(aligned(((part * block + j) * CHUNK + t) * rows + h * HALF, HALF), HALF)
                        total = ys[at, :]
                        for u in range(pair):
                            total = total + (power[u][0] * states[u][j][0] - power[u][1] * states[u][j][1])
                        ys[at, :] = total

    enter(0)
    pl.semaphore_wait(barrier, row_len - 1 + n_rows - 1 + n_ch - 1)
    send_e(0)
    enter(1)
    send_e(1)
    enter(2)
    send_e(2)
    send_t(0)
    enter(3)
    send_e(3)
    send_t(1)
    near(0)
    send_t(2)
    send_s(0)
    near(1)
    send_t(3)
    send_s(1)
    prepare(0)
    prepare(1)
    send_s(2)
    prepare(2)
    prepare(3)
    send_s(3)
    for g in range(groups):
        far(g)

    q_load.wait()
    lane = lax.broadcasted_iota(jnp.int32, (16, LANES), 1)

    def gate(g, power):
        toks = pl.ds(aligned(g * 16, 16), 16)
        squares = jnp.zeros((16, LANES), F32)
        for r in range(rows):
            lanes = pl.ds(r * LANES, LANES)
            at = pl.ds(g * (16 * rows) + r, 16, stride=rows)
            gated = q_buf[toks, lanes].astype(F32) * ys[at, :]
            gated_ref[pl.ds(aligned((g * rows + r) * 16, 16), 16), :] = gated
            squares = squares + gated * gated
        return jnp.where(lane == g, jnp.sum(squares, axis=1, keepdims=True), power)

    p_all[my_ch] = lax.fori_loop(0, tokens // 16, gate, jnp.zeros((16, LANES), F32))

    def remote_p(dst, src):
        return pltpu.make_async_remote_copy(
            src_ref=p_all.at[src],
            dst_ref=p_all.at[src],
            send_sem=p_send.at[dst],
            recv_sem=p_recv.at[src],
            device_id={"ch": dst},
            device_id_type=MESH_IDS,
        )

    for step in range(1, n_ch):
        remote_p(lax.rem(my_ch + step, n_ch), my_ch).start()

    @pl.loop(0, groups)
    def _(g):
        @pl.loop(1, row_len)
        def _(step):
            k = other_k(step)
            remote_e(g, k).wait_send()

            @pl.when(my_row + k > 0)
            def _():
                remote_s(g, k).wait_send()

        @pl.loop(1, n_rows)
        def _(step):
            @pl.when(my_row + step < n_rows)
            def _():
                remote_t(g, my_row + step).wait_send()

    for step in range(1, n_ch):
        other = lax.rem(my_ch + step, n_ch)
        remote_p(other, other).wait_recv()
    total = p_all[0]
    for c in range(1, n_ch):
        total = total + p_all[c]
    scale_ref[...] = lax.rsqrt(total * (1.0 / (rows * LANES * n_ch)) + EPS)

    for step in range(1, n_ch):
        remote_p(lax.rem(my_ch + step, n_ch), my_ch).wait_send()


def finish_kernel(gated_ref, scale_ref, gain_ref, out_hbm, out_buf, sems):
    tokens, width = out_buf.shape
    rows = width // LANES
    parts = sems.shape[0]
    per_part = tokens // parts // 16
    lane = lax.broadcasted_iota(jnp.int32, (16, LANES), 1)
    stores = []
    for n in range(parts):

        @pl.loop(n * per_part, (n + 1) * per_part)
        def _(g):
            toks = pl.ds(aligned(g * 16, 16), 16)
            scale = jnp.sum(jnp.where(lane == g, scale_ref[...], 0.0), axis=1, keepdims=True)
            scale = jnp.broadcast_to(scale, (16, LANES))
            for r in range(rows):
                lanes = pl.ds(r * LANES, LANES)
                gated = gated_ref[pl.ds(aligned((g * rows + r) * 16, 16), 16), :]
                out_buf[toks, lanes] = (gated * gain_ref[:, lanes] * scale).astype(out_buf.dtype)

        toks = pl.ds(n * (tokens // parts), tokens // parts)
        stores.append(pltpu.make_async_copy(out_buf.at[toks], out_hbm.at[toks], sems.at[n]))
        stores[-1].start()
    for store in stores:
        store.wait()


def per_device(n_seq, n_ch, row_len, query, key, value, decay, angle, res_re, res_im, skip, gain):
    tokens, width = query.shape
    rows = width // LANES
    halves = rows // HALF
    slices = MODES * halves
    chunks = tokens // CHUNK
    n_rows = n_seq // row_len
    groups = slices // row_len
    if groups != 4 or rows != 16 or chunks != 16 or halves != 2:
        raise ValueError("unsupported sizes")
    tile = (HALF, LANES)
    anywhere = pl.BlockSpec(memory_space=pl.ANY)
    vmem = pl.BlockSpec(memory_space=pltpu.VMEM)
    dma = pltpu.SemaphoreType.DMA
    operands = (query, key, value, decay, angle, res_re, res_im, skip.reshape(rows, LANES))
    gated, scale = pl.pallas_call(
        functools.partial(exchange_kernel, n_seq, n_ch, row_len),
        out_shape=(pltpu.VMEM((tokens * rows, LANES), F32), pltpu.VMEM((16, LANES), F32)),
        in_specs=[anywhere] * 8,
        out_specs=(vmem, vmem),
        scratch_shapes=[
            pltpu.VMEM((tokens, width), jnp.bfloat16),
            pltpu.VMEM((tokens, width), jnp.bfloat16),
            pltpu.VMEM((tokens, width), jnp.bfloat16),
            pltpu.VMEM((4, MODES, width), F32),
            pltpu.VMEM((rows, LANES), F32),
            pltpu.VMEM((tokens * rows, LANES), F32),
            pltpu.VMEM((tokens * rows, LANES), F32),
            pltpu.VMEM((6, MODES * rows, LANES), F32),
            pltpu.VMEM((CHUNK, halves) + tile, F32),
            pltpu.VMEM((slices, chunks, 2) + tile, F32),
            pltpu.VMEM((slices, CHUNK, 2) + tile, F32),
            pltpu.VMEM((slices, 4, 2) + tile, F32),
            pltpu.VMEM((slices, 2) + tile, F32),
            pltpu.VMEM((groups, row_len, 2) + tile, F32),
            pltpu.VMEM((groups, 2) + tile, F32),
            pltpu.VMEM((groups, n_rows, 2) + tile, F32),
            pltpu.VMEM((groups, row_len, 2) + tile, F32),
            pltpu.VMEM((slices, 2) + tile, F32),
            pltpu.VMEM((n_ch, 16, LANES), F32),
            dma((5,)),
            dma((2, 4)),
            dma(()),
            dma((groups, row_len)),
            dma((groups, row_len)),
            dma((groups, n_rows)),
            dma((groups, n_rows)),
            dma((groups, row_len)),
            dma((groups, row_len)),
            dma((n_ch,)),
            dma((n_ch,)),
        ],
        compiler_params=pltpu.CompilerParams(collective_id=0, has_side_effects=True, vmem_limit_bytes=40 << 20),
    )(*(pltpu.with_memory_space_constraint(a, pltpu.HBM) for a in operands))
    gated = pltpu.with_memory_space_constraint(gated, pltpu.VMEM)
    scale = pltpu.with_memory_space_constraint(scale, pltpu.VMEM)
    return pl.pallas_call(
        finish_kernel,
        out_shape=jax.ShapeDtypeStruct((tokens, width), jnp.bfloat16),
        in_specs=[vmem, vmem, vmem],
        out_specs=anywhere,
        scratch_shapes=[pltpu.VMEM((tokens, width), jnp.bfloat16), dma((4,))],
        compiler_params=pltpu.CompilerParams(vmem_limit_bytes=8 << 20),
    )(gated, scale, gain.reshape(1, width))


def solution(mesh):
    in_specs = (
        P("seq", "ch"),
        P("seq", "ch"),
        P("seq", "ch"),
        P(None, "ch"),
        P(None, "ch"),
        P(None, "ch"),
        P(None, "ch"),
        P("ch"),
        P("ch"),
    )
    return jax.shard_map(
        functools.partial(per_device, mesh.shape["seq"], mesh.shape["ch"], ROW_LEN),
        mesh=mesh,
        in_specs=in_specs,
        out_specs=P("seq", "ch"),
        check_vma=False,
    )
```

```python
import functools
import math

import jax
import jax.numpy as jnp
from jax import lax
from jax.experimental import pallas as pl
from jax.experimental.pallas import tpu as pltpu
from jax.sharding import PartitionSpec as P

F32 = jnp.float32
MODES = 16
CHUNK = 16
LANES = 128
HALF = 8
EPS = 1e-05
ROW_LEN = 8
OWNERS = 4
MESH_IDS = pl.DeviceIdType.MESH


def aligned(value, step):
    return pl.multiple_of(value, step)


def cmul(a, b):
    return a[0] * b[0] - a[1] * b[1], a[0] * b[1] + a[1] * b[0]


def csquare(a):
    cross = a[0] * a[1]
    return a[0] * a[0] - a[1] * a[1], cross + cross


def cadd(a, b):
    return a[0] + b[0], a[1] + b[1]


def sin_cos(angle):
    z = angle * 0.5
    w = z * z
    s = jnp.full_like(w, 1.0 / math.factorial(13))
    for n in (11, 9, 7, 5, 3, 1):
        s = s * w + ((-1.0) ** ((n - 1) // 2)) / math.factorial(n)
    s = s * z
    c = jnp.full_like(w, 1.0 / math.factorial(12))
    for n in (10, 8, 6, 4, 2, 0):
        c = c * w + ((-1.0) ** (n // 2)) / math.factorial(n)
    sc = s * c
    return sc + sc, 1.0 - 2.0 * (s * s)


def whole_power(decay, angle, count):
    v = angle * float(count)
    turns = jnp.floor(v * (0.5 / math.pi) + 0.5)
    first = 6.28125
    second = round((2.0 * math.pi - first) * 2.0**23) / 2.0**23
    third = 2.0 * math.pi - first - second
    rest = ((v - turns * first) - turns * second) - turns * third
    s, c = sin_cos(rest)
    magnitude = jnp.exp(decay * -float(count))
    return magnitude * c, magnitude * s


def exchange_kernel(
    n_seq,
    n_ch,
    row_len,
    q_hbm,
    k_hbm,
    v_hbm,
    decay_hbm,
    angle_hbm,
    res_re_hbm,
    res_im_hbm,
    skip_hbm,
    gated_ref,
    scale_ref,
    q_buf,
    k_buf,
    v_buf,
    raw,
    skip_buf,
    xs,
    ys,
    par,
    taps,
    zs,
    table,
    qpow,
    e_stage,
    e_row,
    t_out,
    t_all,
    s_out,
    s_all,
    p_all,
    raw_sems,
    kv_sems,
    q_sem,
    e_send,
    e_recv,
    t_send,
    t_recv,
    s_send,
    s_recv,
    p_send,
    p_recv,
):
    me = lax.axis_index("seq")
    my_ch = lax.axis_index("ch")
    my_row = me // row_len
    my_k = lax.rem(me, row_len)
    n_rows = n_seq // row_len
    tokens = q_buf.shape[0]
    rows = q_buf.shape[1] // LANES
    chunks = tokens // CHUNK
    halves = rows // HALF
    slices = MODES * halves
    groups = MODES // OWNERS

    raw_loads = [
        pltpu.make_async_copy(src, raw.at[n], raw_sems.at[n])
        for n, src in enumerate((decay_hbm, angle_hbm, res_re_hbm, res_im_hbm))
    ]
    raw_loads.append(pltpu.make_async_copy(skip_hbm, skip_buf, raw_sems.at[4]))
    for load in raw_loads:
        load.start()
    parts = kv_sems.shape[1]
    kv_loads = []
    for n in range(parts):
        toks = pl.ds(n * (tokens // parts), tokens // parts)
        kv_loads.append(
            [
                pltpu.make_async_copy(k_hbm.at[toks], k_buf.at[toks], kv_sems.at[0, n]),
                pltpu.make_async_copy(v_hbm.at[toks], v_buf.at[toks], kv_sems.at[1, n]),
            ]
        )
        for load in kv_loads[-1]:
            load.start()
    q_load = pltpu.make_async_copy(q_hbm, q_buf, q_sem)

    def in_row(k):
        return {"seq": my_row * row_len + k}

    def other_k(step):
        return lax.rem(my_k + step, row_len)

    barrier = pltpu.get_barrier_semaphore()

    @pl.loop(1, row_len)
    def _(step):
        pl.semaphore_signal(barrier, inc=1, device_id=in_row(other_k(step)), device_id_type=MESH_IDS)

    @pl.loop(1, n_rows)
    def _(step):
        row = lax.rem(my_row + step, n_rows)
        pl.semaphore_signal(barrier, inc=1, device_id={"seq": row * row_len + my_k}, device_id_type=MESH_IDS)

    @pl.loop(1, n_ch)
    def _(step):
        pl.semaphore_signal(barrier, inc=1, device_id={"ch": lax.rem(my_ch + step, n_ch)}, device_id_type=MESH_IDS)

    for load in raw_loads:
        load.wait()

    @pl.loop(0, rows)
    def _(r):
        lanes = pl.ds(aligned(r * LANES, LANES), LANES)
        place = pl.ds(r, MODES, stride=rows)
        decay = raw[0, :, lanes]
        angle = raw[1, :, lanes]
        s, c = sin_cos(angle)
        magnitude = jnp.exp(-decay)
        weight = jnp.sqrt(decay)
        par[0, place, :] = magnitude * c
        par[1, place, :] = magnitude * s
        par[2, place, :] = weight * raw[2, :, lanes]
        par[3, place, :] = weight * raw[3, :, lanes]
        par[4, place, :] = decay
        par[5, place, :] = angle

    zero = jnp.zeros((HALF, LANES), F32)
    for h in range(halves):
        taps[0, h] = skip_buf[pl.ds(h * HALF, HALF), :]
        for n in range(1, CHUNK):
            taps[n, h] = zero

    @pl.when(me == 0)
    def _():
        @pl.loop(0, slices)
        def _(i):
            s_all[i, 0] = zero
            s_all[i, 1] = zero

    per_part = tokens // parts // 16
    for n in range(parts):
        for load in kv_loads[n]:
            load.wait()

        @pl.loop(n * per_part, (n + 1) * per_part)
        def _(g):
            toks = pl.ds(aligned(g * 16, 16), 16)
            for r in range(rows):
                lanes = pl.ds(r * LANES, LANES)
                xs[pl.ds(g * (16 * rows) + r, 16, stride=rows), :] = k_buf[toks, lanes].astype(F32) * v_buf[toks, lanes].astype(F32)

    q_load.start()
    is_owner = my_k < OWNERS

    def own_rates(g, h):
        at = pl.ds(aligned((g * OWNERS + my_k) * rows + h * HALF, HALF), HALF)
        return par[4, at, :], par[5, at, :]

    def enter(g):
        @pl.loop(g * row_len, (g + 1) * row_len)
        def _(i):
            m = i // halves
            h = lax.rem(i, halves)
            here = pl.ds(aligned(m * rows + h * HALF, HALF), HALF)
            pole = (par[0, here, :], par[1, here, :])
            w = (par[2, here, :], par[3, here, :])
            z = [None] * chunks
            for n in range(CHUNK):
                taps[n, h] += w[0]
                for j in range(chunks):
                    x = xs[pl.ds(aligned((j * CHUNK + CHUNK - 1 - n) * rows + h * HALF, HALF), HALF), :]
                    term = (w[0] * x, w[1] * x)
                    z[j] = term if n == 0 else cadd(z[j], term)
                if n < CHUNK - 1:
                    w = cmul(w, pole)
            power = pole
            for _ in range(4):
                power = csquare(power)
            for j in range(chunks):
                zs[i, j, 0] = z[j][0]
                zs[i, j, 1] = z[j][1]
            level = 0
            while len(z) > 1:
                qpow[i, level, 0] = power[0]
                qpow[i, level, 1] = power[1]
                z = [cadd(cmul(z[2 * j], power), z[2 * j + 1]) for j in range(len(z) // 2)]
                level += 1
                if len(z) > 1:
                    power = csquare(power)
            e_stage[i, 0] = z[0][0]
            e_stage[i, 1] = z[0][1]

        @pl.when(is_owner)
        def _():
            for h in range(halves):
                e_row[g, my_k, h] = e_stage[(g * OWNERS + my_k) * halves + h]

    def mode_slices(g, k):
        return pl.ds((g * OWNERS + k) * halves, halves)

    def remote_e(g, k):
        return pltpu.make_async_remote_copy(
            src_ref=e_stage.at[mode_slices(g, k)],
            dst_ref=e_row.at[g, my_k],
            send_sem=e_send,
            recv_sem=e_recv.at[g],
            device_id=in_row(k),
            device_id_type=MESH_IDS,
        )

    def remote_t(g, row):
        return pltpu.make_async_remote_copy(
            src_ref=t_out.at[g],
            dst_ref=t_all.at[g * n_rows + my_row],
            send_sem=t_send,
            recv_sem=t_recv.at[g, my_row],
            device_id={"seq": row * row_len + my_k},
            device_id_type=MESH_IDS,
        )

    def remote_s(g, k):
        aside = (n_seq - (my_row * row_len + k)) // n_seq
        return pltpu.make_async_remote_copy(
            src_ref=s_out.at[g * row_len + k],
            dst_ref=s_all.at[pl.ds(aside * slices + (g * OWNERS + my_k) * halves, halves)],
            send_sem=s_send,
            recv_sem=s_recv.at[g],
            device_id=in_row(k),
            device_id_type=MESH_IDS,
        )

    def whole(ref, count, send_sem, recv_sem):
        part = ref.at[pl.ds(0, count)]
        return pltpu.make_async_remote_copy(
            src_ref=part,
            dst_ref=part,
            send_sem=send_sem,
            recv_sem=recv_sem,
            device_id=in_row(other_k(1)),
            device_id_type=MESH_IDS,
        )

    def send_e(g):
        for k in range(OWNERS):

            @pl.when(k != my_k)
            def _():
                remote_e(g, k).start()

    def send_t(g):
        @pl.when(is_owner)
        def _():
            whole(e_row.at[g], row_len - 1, e_send, e_recv.at[g]).wait_recv()
            for h in range(halves):
                jump = whole_power(*own_rates(g, h), tokens)
                total = (e_row[g, 0, h, 0], e_row[g, 0, h, 1])
                for k in range(1, row_len):
                    total = cadd(cmul(total, jump), (e_row[g, k, h, 0], e_row[g, k, h, 1]))
                t_out[g, h, 0] = total[0]
                t_out[g, h, 1] = total[1]
            for row in range(1, n_rows):

                @pl.when(my_row < row)
                def _():
                    remote_t(g, row).start()

    def send_s(g):
        @pl.when(is_owner)
        def _():
            jumps = [whole_power(*own_rates(g, h), tokens) for h in range(halves)]
            row_jumps = [whole_power(*own_rates(g, h), tokens * row_len) for h in range(halves)]

            def add_row(row, states):
                pltpu.make_async_remote_copy(
                    src_ref=t_out.at[g],
                    dst_ref=t_all.at[g * n_rows + row],
                    send_sem=t_send,
                    recv_sem=t_recv.at[g, row],
                    device_id=in_row(other_k(1)),
                    device_id_type=MESH_IDS,
                ).wait_recv()
                at = g * n_rows + row
                return tuple(
                    cadd(cmul(states[h], row_jumps[h]), (t_all[at, h, 0], t_all[at, h, 1])) for h in range(halves)
                )

            states = lax.fori_loop(0, my_row, add_row, ((zero, zero),) * halves)
            for h in range(halves):
                state = states[h]
                for k in range(row_len):
                    s_out[g * row_len + k, h, 0] = state[0]
                    s_out[g * row_len + k, h, 1] = state[1]
                    if k < row_len - 1:
                        state = cadd(cmul(state, jumps[h]), (e_row[g, k, h, 0], e_row[g, k, h, 1]))
            for h in range(halves):
                s_all[(g * OWNERS + my_k) * halves + h] = s_out[g * row_len + my_k, h]
            for step in range(1, row_len):
                remote_s(g, other_k(step)).start()

    def wait_s(g):
        @pl.when(is_owner)
        def _():
            whole(s_all, (OWNERS - 1) * halves, s_send, s_recv.at[g]).wait_recv()

        @pl.when(my_k >= OWNERS)
        def _():
            whole(s_all, OWNERS * halves, s_send, s_recv.at[g]).wait_recv()

    def near(h):
        @pl.loop(0, chunks)
        def _(j):
            tap = [taps[n, h] for n in range(CHUNK)]
            x = [xs[pl.ds(aligned((j * CHUNK + s) * rows + h * HALF, HALF), HALF), :] for s in range(CHUNK)]
            for t in range(CHUNK):
                total = tap[t] * x[0]
                for s in range(1, t + 1):
                    total = total + tap[t - s] * x[s]
                ys[pl.ds(aligned((j * CHUNK + t) * rows + h * HALF, HALF), HALF), :] = total

    def prepare(g):
        unit = 4

        @pl.loop(0, row_len // unit)
        def _(b):
            ids = [g * row_len + b * unit + u for u in range(unit)]
            step = [(qpow[i, 0, 0], qpow[i, 0, 1]) for i in ids]
            states = [(zs[i, 0, 0], zs[i, 0, 1]) for i in ids]
            poles = []
            for i in ids:
                here = pl.ds(aligned((i // halves) * rows + lax.rem(i, halves) * HALF, HALF), HALF)
                poles.append((par[0, here, :], par[1, here, :]))
            powers = list(poles)
            for j in range(1, chunks):
                for u, i in enumerate(ids):
                    if j < chunks - 1:
                        following = cadd(cmul(states[u], step[u]), (zs[i, j, 0], zs[i, j, 1]))
                    zs[i, j, 0] = states[u][0]
                    zs[i, j, 1] = states[u][1]
                    if j < chunks - 1:
                        states[u] = following
            for t in range(CHUNK):
                for u, i in enumerate(ids):
                    table[i, t, 0] = powers[u][0]
                    table[i, t, 1] = powers[u][1]
                    if t < CHUNK - 1:
                        powers[u] = cmul(powers[u], poles[u])

    pair = 2
    block = chunks // 2

    def far(g):
        @pl.when(me > 0)
        def _():
            wait_s(g)

        @pl.loop(0, row_len // pair)
        def _(b):
            h = lax.rem(b, halves)
            first = g * row_len + (b // halves) * (pair * halves) + h
            ids = [first + u * halves for u in range(pair)]
            starts = []
            for i in ids:
                d = [(s_all[i, 0], s_all[i, 1])]
                for level in range(3):
                    power = (qpow[i, level, 0], qpow[i, level, 1])
                    d = d + [cmul(a, power) for a in d]
                starts.append(d)
            for part in range(2):
                states = []
                for u, i in enumerate(ids):
                    if part == 1:
                        power = (qpow[i, 3, 0], qpow[i, 3, 1])
                        starts[u] = [cmul(a, power) for a in starts[u]]
                    states.append(
                        [
                            starts[u][j]
                            if part == 0 and j == 0
                            else cadd(starts[u][j], (zs[i, part * block + j, 0], zs[i, part * block + j, 1]))
                            for j in range(block)
                        ]
                    )
                for t in range(CHUNK):
                    power = [(table[i, t, 0], table[i, t, 1]) for i in ids]
                    for j in range(block):
                        at = pl.ds(aligned(((part * block + j) * CHUNK + t) * rows + h * HALF, HALF), HALF)
                        total = ys[at, :]
                        for u in range(pair):
                            total = total + (power[u][0] * states[u][j][0] - power[u][1] * states[u][j][1])
                        ys[at, :] = total

    enter(0)
    pl.semaphore_wait(barrier, row_len - 1 + n_rows - 1 + n_ch - 1)
    send_e(0)
    enter(1)
    send_e(1)
    enter(2)
    send_e(2)
    enter(3)
    send_e(3)
    send_t(0)
    near(0)
    send_t(1)
    near(1)
    send_t(2)
    send_s(0)
    prepare(0)
    prepare(1)
    send_s(1)
    send_t(3)
    prepare(2)
    prepare(3)
    send_s(2)
    far(0)
    send_s(3)
    far(1)
    far(2)
    far(3)

    q_load.wait()
    lane = lax.broadcasted_iota(jnp.int32, (16, LANES), 1)

    @pl.loop(0, tokens // 16)
    def _(g):
        toks = pl.ds(aligned(g * 16, 16), 16)
        squares = jnp.zeros((16, LANES), F32)
        for r in range(rows):
            lanes = pl.ds(r * LANES, LANES)
            at = pl.ds(g * (16 * rows) + r, 16, stride=rows)
            gated = q_buf[toks, lanes].astype(F32) * ys[at, :]
            gated_ref[pl.ds(aligned((g * rows + r) * 16, 16), 16), :] = gated
            squares = squares + gated * gated
        xs[toks, :] = squares

    power = jnp.zeros((16, LANES), F32)
    for g in range(tokens // 16):
        squares = xs[pl.ds(g * 16, 16), :]
        power = jnp.where(lane == g, jnp.sum(squares, axis=1, keepdims=True), power)
    p_all[my_ch] = power

    def remote_p(dst):
        return pltpu.make_async_remote_copy(
            src_ref=p_all.at[my_ch],
            dst_ref=p_all.at[my_ch],
            send_sem=p_send,
            recv_sem=p_recv,
            device_id={"ch": dst},
            device_id_type=MESH_IDS,
        )

    for step in range(1, n_ch):
        remote_p(lax.rem(my_ch + step, n_ch)).start()

    @pl.when(is_owner)
    def _():
        whole(e_stage, (OWNERS - 1) * halves * groups, e_send, e_recv.at[0]).wait_send()
        whole(s_out, (row_len - 1) * groups, s_send, s_recv.at[0]).wait_send()
        for row in range(n_rows - 1):

            @pl.when(my_row == row)
            def _():
                whole(t_all, (n_rows - 1 - row) * groups, t_send, t_recv.at[0, 0]).wait_send()

    @pl.when(my_k >= OWNERS)
    def _():
        whole(e_stage, OWNERS * halves * groups, e_send, e_recv.at[0]).wait_send()

    @pl.when(me == 0)
    def _():
        for g in range(groups):
            wait_s(g)

    others = whole(p_all, n_ch - 1, p_send, p_recv)
    others.wait_recv()
    total = p_all[0]
    for c in range(1, n_ch):
        total = total + p_all[c]
    scale_ref[...] = lax.rsqrt(total * (1.0 / (rows * LANES * n_ch)) + EPS)
    others.wait_send()


def finish_kernel(gated_ref, scale_ref, gain_ref, out_hbm, out_buf, sems):
    tokens, width = out_buf.shape
    rows = width // LANES
    parts = sems.shape[0]
    per_part = tokens // parts // 16
    lane = lax.broadcasted_iota(jnp.int32, (16, LANES), 1)
    stores = []
    for n in range(parts):

        @pl.loop(n * per_part, (n + 1) * per_part)
        def _(g):
            toks = pl.ds(aligned(g * 16, 16), 16)
            scale = jnp.sum(jnp.where(lane == g, scale_ref[...], 0.0), axis=1, keepdims=True)
            scale = jnp.broadcast_to(scale, (16, LANES))
            for r in range(rows):
                lanes = pl.ds(r * LANES, LANES)
                gated = gated_ref[pl.ds(aligned((g * rows + r) * 16, 16), 16), :]
                out_buf[toks, lanes] = (gated * gain_ref[:, lanes] * scale).astype(out_buf.dtype)

        toks = pl.ds(n * (tokens // parts), tokens // parts)
        stores.append(pltpu.make_async_copy(out_buf.at[toks], out_hbm.at[toks], sems.at[n]))
        stores[-1].start()
    for store in stores:
        store.wait()


def per_device(n_seq, n_ch, row_len, query, key, value, decay, angle, res_re, res_im, skip, gain):
    tokens, width = query.shape
    rows = width // LANES
    halves = rows // HALF
    slices = MODES * halves
    chunks = tokens // CHUNK
    n_rows = n_seq // row_len
    groups = MODES // OWNERS
    if groups != 4 or slices != groups * row_len or rows != 16 or chunks != 16 or halves != 2:
        raise ValueError("unsupported sizes")
    tile = (HALF, LANES)
    anywhere = pl.BlockSpec(memory_space=pl.ANY)
    vmem = pl.BlockSpec(memory_space=pltpu.VMEM)
    dma = pltpu.SemaphoreType.DMA
    operands = (query, key, value, decay, angle, res_re, res_im, skip.reshape(rows, LANES))
    gated, scale = pl.pallas_call(
        functools.partial(exchange_kernel, n_seq, n_ch, row_len),
        out_shape=(pltpu.VMEM((tokens * rows, LANES), F32), pltpu.VMEM((16, LANES), F32)),
        in_specs=[anywhere] * 8,
        out_specs=(vmem, vmem),
        scratch_shapes=[
            pltpu.VMEM((tokens, width), jnp.bfloat16),
            pltpu.VMEM((tokens, width), jnp.bfloat16),
            pltpu.VMEM((tokens, width), jnp.bfloat16),
            pltpu.VMEM((4, MODES, width), F32),
            pltpu.VMEM((rows, LANES), F32),
            pltpu.VMEM((tokens * rows, LANES), F32),
            pltpu.VMEM((tokens * rows, LANES), F32),
            pltpu.VMEM((6, MODES * rows, LANES), F32),
            pltpu.VMEM((CHUNK, halves) + tile, F32),
            pltpu.VMEM((slices, chunks, 2) + tile, F32),
            pltpu.VMEM((slices, CHUNK, 2) + tile, F32),
            pltpu.VMEM((slices, 4, 2) + tile, F32),
            pltpu.VMEM((slices, 2) + tile, F32),
            pltpu.VMEM((groups, row_len, halves, 2) + tile, F32),
            pltpu.VMEM((groups, halves, 2) + tile, F32),
            pltpu.VMEM((groups * n_rows, halves, 2) + tile, F32),
            pltpu.VMEM((groups * row_len, halves, 2) + tile, F32),
            pltpu.VMEM((2 * slices, 2) + tile, F32),
            pltpu.VMEM((n_ch, 16, LANES), F32),
            dma((5,)),
            dma((2, 4)),
            dma(()),
            dma(()),
            dma((groups,)),
            dma(()),
            dma((groups, n_rows)),
            dma(()),
            dma((groups,)),
            dma(()),
            dma(()),
        ],
        compiler_params=pltpu.CompilerParams(collective_id=0, has_side_effects=True, vmem_limit_bytes=40 << 20),
    )(*(pltpu.with_memory_space_constraint(a, pltpu.HBM) for a in operands))
    gated = pltpu.with_memory_space_constraint(gated, pltpu.VMEM)
    scale = pltpu.with_memory_space_constraint(scale, pltpu.VMEM)
    return pl.pallas_call(
        finish_kernel,
        out_shape=jax.ShapeDtypeStruct((tokens, width), jnp.bfloat16),
        in_specs=[vmem, vmem, vmem],
        out_specs=anywhere,
        scratch_shapes=[pltpu.VMEM((tokens, width), jnp.bfloat16), dma((4,))],
        compiler_params=pltpu.CompilerParams(vmem_limit_bytes=8 << 20),
    )(gated, scale, gain.reshape(1, width))


def solution(mesh):
    in_specs = (
        P("seq", "ch"),
        P("seq", "ch"),
        P("seq", "ch"),
        P(None, "ch"),
        P(None, "ch"),
        P(None, "ch"),
        P(None, "ch"),
        P("ch"),
        P("ch"),
    )
    return jax.shard_map(
        functools.partial(per_device, mesh.shape["seq"], mesh.shape["ch"], ROW_LEN),
        mesh=mesh,
        in_specs=in_specs,
        out_specs=P("seq", "ch"),
        check_vma=False,
    )
```

```python
import functools
import math

import jax
import jax.numpy as jnp
from jax import lax
from jax.experimental import pallas as pl
from jax.experimental.pallas import tpu as pltpu
from jax.sharding import PartitionSpec as P

F32 = jnp.float32
MODES = 16
CHUNK = 16
LANES = 128
HALF = 8
EPS = 1e-05
ROW_LEN = 8
OWNERS = 4
MESH_IDS = pl.DeviceIdType.MESH


def aligned(value, step):
    return pl.multiple_of(value, step)


def cmul(a, b):
    return a[0] * b[0] - a[1] * b[1], a[0] * b[1] + a[1] * b[0]


def csquare(a):
    cross = a[0] * a[1]
    return a[0] * a[0] - a[1] * a[1], cross + cross


def cadd(a, b):
    return a[0] + b[0], a[1] + b[1]


def sin_cos(angle):
    z = angle * 0.5
    w = z * z
    s = jnp.full_like(w, 1.0 / math.factorial(13))
    for n in (11, 9, 7, 5, 3, 1):
        s = s * w + ((-1.0) ** ((n - 1) // 2)) / math.factorial(n)
    s = s * z
    c = jnp.full_like(w, 1.0 / math.factorial(12))
    for n in (10, 8, 6, 4, 2, 0):
        c = c * w + ((-1.0) ** (n // 2)) / math.factorial(n)
    sc = s * c
    return sc + sc, 1.0 - 2.0 * (s * s)


def whole_power(decay, angle, count):
    v = angle * float(count)
    turns = jnp.floor(v * (0.5 / math.pi) + 0.5)
    first = 6.28125
    second = round((2.0 * math.pi - first) * 2.0**23) / 2.0**23
    third = 2.0 * math.pi - first - second
    rest = ((v - turns * first) - turns * second) - turns * third
    s, c = sin_cos(rest)
    magnitude = jnp.exp(decay * -float(count))
    return magnitude * c, magnitude * s


def exchange_kernel(
    n_seq,
    n_ch,
    row_len,
    q_hbm,
    k_hbm,
    v_hbm,
    decay_hbm,
    angle_hbm,
    res_re_hbm,
    res_im_hbm,
    skip_hbm,
    gated_ref,
    scale_ref,
    q_buf,
    k_buf,
    v_buf,
    raw,
    skip_buf,
    xs,
    ys,
    par,
    taps,
    zs,
    table,
    qpow,
    e_stage,
    e_row,
    t_out,
    t_all,
    s_out,
    s_all,
    p_all,
    jumps_ref,
    raw_sems,
    kv_sems,
    q_sem,
    e_send,
    e_recv,
    t_send,
    t_recv,
    s_send,
    s_recv,
    p_send,
    p_recv,
):
    me = lax.axis_index("seq")
    my_ch = lax.axis_index("ch")
    my_row = me // row_len
    my_k = lax.rem(me, row_len)
    n_rows = n_seq // row_len
    tokens = q_buf.shape[0]
    rows = q_buf.shape[1] // LANES
    chunks = tokens // CHUNK
    halves = rows // HALF
    slices = MODES * halves
    groups = MODES // OWNERS

    raw_loads = [
        pltpu.make_async_copy(src, raw.at[n], raw_sems.at[n])
        for n, src in enumerate((decay_hbm, angle_hbm, res_re_hbm, res_im_hbm))
    ]
    raw_loads.append(pltpu.make_async_copy(skip_hbm, skip_buf, raw_sems.at[4]))
    for load in raw_loads:
        load.start()
    parts = kv_sems.shape[1]
    kv_loads = []
    for n in range(parts):
        toks = pl.ds(n * (tokens // parts), tokens // parts)
        kv_loads.append(
            [
                pltpu.make_async_copy(k_hbm.at[toks], k_buf.at[toks], kv_sems.at[0, n]),
                pltpu.make_async_copy(v_hbm.at[toks], v_buf.at[toks], kv_sems.at[1, n]),
            ]
        )
        for load in kv_loads[-1]:
            load.start()
    q_load = pltpu.make_async_copy(q_hbm, q_buf, q_sem)

    def in_row(k):
        return {"seq": my_row * row_len + k}

    def other_k(step):
        return lax.rem(my_k + step, row_len)

    barrier = pltpu.get_barrier_semaphore()

    @pl.loop(1, row_len)
    def _(step):
        pl.semaphore_signal(barrier, inc=1, device_id=in_row(other_k(step)), device_id_type=MESH_IDS)

    @pl.loop(1, n_rows)
    def _(step):
        row = lax.rem(my_row + step, n_rows)
        pl.semaphore_signal(barrier, inc=1, device_id={"seq": row * row_len + my_k}, device_id_type=MESH_IDS)

    @pl.loop(1, n_ch)
    def _(step):
        pl.semaphore_signal(barrier, inc=1, device_id={"ch": lax.rem(my_ch + step, n_ch)}, device_id_type=MESH_IDS)

    for load in raw_loads:
        load.wait()

    @pl.loop(0, rows)
    def _(r):
        lanes = pl.ds(aligned(r * LANES, LANES), LANES)
        place = pl.ds(r, MODES, stride=rows)
        decay = raw[0, :, lanes]
        angle = raw[1, :, lanes]
        s, c = sin_cos(angle)
        magnitude = jnp.exp(-decay)
        weight = jnp.sqrt(decay)
        par[0, place, :] = magnitude * c
        par[1, place, :] = magnitude * s
        par[2, place, :] = weight * raw[2, :, lanes]
        par[3, place, :] = weight * raw[3, :, lanes]
        par[4, place, :] = decay
        par[5, place, :] = angle

    zero = jnp.zeros((HALF, LANES), F32)
    for h in range(halves):
        taps[0, h] = skip_buf[pl.ds(h * HALF, HALF), :]
        for n in range(1, CHUNK):
            taps[n, h] = zero

    @pl.when(me == 0)
    def _():
        @pl.loop(0, slices)
        def _(i):
            s_all[i, 0] = zero
            s_all[i, 1] = zero

    is_owner = my_k < OWNERS

    @pl.when(is_owner)
    def _():
        for g in range(groups):
            for h in range(halves):
                at = pl.ds(aligned((g * OWNERS + my_k) * rows + h * HALF, HALF), HALF)
                for n, count in enumerate((tokens, tokens * row_len)):
                    jump = whole_power(par[4, at, :], par[5, at, :], count)
                    jumps_ref[g, h, n, 0] = jump[0]
                    jumps_ref[g, h, n, 1] = jump[1]

    per_part = tokens // parts // 16
    for n in range(parts):
        for load in kv_loads[n]:
            load.wait()

        @pl.loop(n * per_part, (n + 1) * per_part)
        def _(g):
            toks = pl.ds(aligned(g * 16, 16), 16)
            for r in range(rows):
                lanes = pl.ds(r * LANES, LANES)
                xs[pl.ds(g * (16 * rows) + r, 16, stride=rows), :] = k_buf[toks, lanes].astype(F32) * v_buf[toks, lanes].astype(F32)

    q_load.start()

    def jumps(g, n):
        return [(jumps_ref[g, h, n, 0], jumps_ref[g, h, n, 1]) for h in range(halves)]

    def enter(g):
        @pl.loop(g * row_len, (g + 1) * row_len)
        def _(i):
            m = i // halves
            h = lax.rem(i, halves)
            here = pl.ds(aligned(m * rows + h * HALF, HALF), HALF)
            pole = (par[0, here, :], par[1, here, :])
            w = (par[2, here, :], par[3, here, :])
            z = [None] * chunks
            for n in range(CHUNK):
                taps[n, h] += w[0]
                for j in range(chunks):
                    x = xs[pl.ds(aligned((j * CHUNK + CHUNK - 1 - n) * rows + h * HALF, HALF), HALF), :]
                    term = (w[0] * x, w[1] * x)
                    z[j] = term if n == 0 else cadd(z[j], term)
                if n < CHUNK - 1:
                    w = cmul(w, pole)
            power = pole
            for _ in range(4):
                power = csquare(power)
            for j in range(chunks):
                zs[i, j, 0] = z[j][0]
                zs[i, j, 1] = z[j][1]
            level = 0
            while len(z) > 1:
                qpow[i, level, 0] = power[0]
                qpow[i, level, 1] = power[1]
                z = [cadd(cmul(z[2 * j], power), z[2 * j + 1]) for j in range(len(z) // 2)]
                level += 1
                if len(z) > 1:
                    power = csquare(power)
            e_stage[i, 0] = z[0][0]
            e_stage[i, 1] = z[0][1]

        @pl.when(is_owner)
        def _():
            for h in range(halves):
                e_row[g, my_k, h] = e_stage[(g * OWNERS + my_k) * halves + h]

    def mode_slices(g, k):
        return pl.ds((g * OWNERS + k) * halves, halves)

    def remote_e(g, k):
        return pltpu.make_async_remote_copy(
            src_ref=e_stage.at[mode_slices(g, k)],
            dst_ref=e_row.at[g, my_k],
            send_sem=e_send,
            recv_sem=e_recv.at[g],
            device_id=in_row(k),
            device_id_type=MESH_IDS,
        )

    def remote_t(g, row):
        return pltpu.make_async_remote_copy(
            src_ref=t_out.at[g],
            dst_ref=t_all.at[g * n_rows + my_row],
            send_sem=t_send,
            recv_sem=t_recv.at[g, my_row],
            device_id={"seq": row * row_len + my_k},
            device_id_type=MESH_IDS,
        )

    def remote_s(g, k):
        aside = (n_seq - (my_row * row_len + k)) // n_seq
        return pltpu.make_async_remote_copy(
            src_ref=s_out.at[g * row_len + k],
            dst_ref=s_all.at[pl.ds(aside * slices + (g * OWNERS + my_k) * halves, halves)],
            send_sem=s_send,
            recv_sem=s_recv.at[g, my_k // halves],
            device_id=in_row(k),
            device_id_type=MESH_IDS,
        )

    def whole(ref, count, send_sem, recv_sem):
        part = ref.at[pl.ds(0, count)]
        return pltpu.make_async_remote_copy(
            src_ref=part,
            dst_ref=part,
            send_sem=send_sem,
            recv_sem=recv_sem,
            device_id=in_row(other_k(1)),
            device_id_type=MESH_IDS,
        )

    def send_e(g):
        for k in range(OWNERS):

            @pl.when(k != my_k)
            def _():
                remote_e(g, k).start()

    def send_t(g):
        @pl.when(is_owner)
        def _():
            whole(e_row.at[g], row_len - 1, e_send, e_recv.at[g]).wait_recv()
            jump = jumps(g, 0)
            for h in range(halves):
                total = (e_row[g, 0, h, 0], e_row[g, 0, h, 1])
                for k in range(1, row_len):
                    total = cadd(cmul(total, jump[h]), (e_row[g, k, h, 0], e_row[g, k, h, 1]))
                t_out[g, h, 0] = total[0]
                t_out[g, h, 1] = total[1]
            for row in range(1, n_rows):

                @pl.when(my_row < row)
                def _():
                    remote_t(g, row).start()

    def send_s(g):
        @pl.when(is_owner)
        def _():
            jump, row_jump = jumps(g, 0), jumps(g, 1)

            def add_row(row, states):
                pltpu.make_async_remote_copy(
                    src_ref=t_out.at[g],
                    dst_ref=t_all.at[g * n_rows + row],
                    send_sem=t_send,
                    recv_sem=t_recv.at[g, row],
                    device_id=in_row(other_k(1)),
                    device_id_type=MESH_IDS,
                ).wait_recv()
                at = g * n_rows + row
                return tuple(
                    cadd(cmul(states[h], row_jump[h]), (t_all[at, h, 0], t_all[at, h, 1])) for h in range(halves)
                )

            states = lax.fori_loop(0, my_row, add_row, ((zero, zero),) * halves)
            for h in range(halves):
                state = states[h]
                for k in range(row_len):
                    s_out[g * row_len + k, h, 0] = state[0]
                    s_out[g * row_len + k, h, 1] = state[1]
                    if k < row_len - 1:
                        state = cadd(cmul(state, jump[h]), (e_row[g, k, h, 0], e_row[g, k, h, 1]))
            for h in range(halves):
                s_all[(g * OWNERS + my_k) * halves + h] = s_out[g * row_len + my_k, h]
            for step in range(1, row_len):
                remote_s(g, other_k(step)).start()

    def wait_s(g, part):
        @pl.when(my_k // halves == part)
        def _():
            whole(s_all, halves, s_send, s_recv.at[g, part]).wait_recv()

        @pl.when(my_k // halves != part)
        def _():
            whole(s_all, halves * halves, s_send, s_recv.at[g, part]).wait_recv()

    def near(h):
        @pl.loop(0, chunks)
        def _(j):
            tap = [taps[n, h] for n in range(CHUNK)]
            x = [xs[pl.ds(aligned((j * CHUNK + s) * rows + h * HALF, HALF), HALF), :] for s in range(CHUNK)]
            for t in range(CHUNK):
                total = tap[t] * x[0]
                for s in range(1, t + 1):
                    total = total + tap[t - s] * x[s]
                ys[pl.ds(aligned((j * CHUNK + t) * rows + h * HALF, HALF), HALF), :] = total

    def prepare(g):
        unit = 4

        @pl.loop(0, row_len // unit)
        def _(b):
            ids = [g * row_len + b * unit + u for u in range(unit)]
            step = [(qpow[i, 0, 0], qpow[i, 0, 1]) for i in ids]
            states = [(zs[i, 0, 0], zs[i, 0, 1]) for i in ids]
            poles = []
            for i in ids:
                here = pl.ds(aligned((i // halves) * rows + lax.rem(i, halves) * HALF, HALF), HALF)
                poles.append((par[0, here, :], par[1, here, :]))
            powers = list(poles)
            for j in range(1, chunks):
                for u, i in enumerate(ids):
                    if j < chunks - 1:
                        following = cadd(cmul(states[u], step[u]), (zs[i, j, 0], zs[i, j, 1]))
                    zs[i, j, 0] = states[u][0]
                    zs[i, j, 1] = states[u][1]
                    if j < chunks - 1:
                        states[u] = following
            for t in range(CHUNK):
                for u, i in enumerate(ids):
                    table[i, t, 0] = powers[u][0]
                    table[i, t, 1] = powers[u][1]
                    if t < CHUNK - 1:
                        powers[u] = cmul(powers[u], poles[u])

    pair = 2
    block = chunks // 2

    def far(g):
        @pl.loop(0, row_len // pair)
        def _(b):
            @pl.when((me > 0) & (lax.rem(b, halves) == 0))
            def _():
                wait_s(g, b // halves)

            h = lax.rem(b, halves)
            first = g * row_len + (b // halves) * (pair * halves) + h
            ids = [first + u * halves for u in range(pair)]
            starts = []
            for i in ids:
                d = [(s_all[i, 0], s_all[i, 1])]
                for level in range(3):
                    power = (qpow[i, level, 0], qpow[i, level, 1])
                    d = d + [cmul(a, power) for a in d]
                starts.append(d)
            for part in range(2):
                states = []
                for u, i in enumerate(ids):
                    if part == 1:
                        power = (qpow[i, 3, 0], qpow[i, 3, 1])
                        starts[u] = [cmul(a, power) for a in starts[u]]
                    states.append(
                        [
                            starts[u][j]
                            if part == 0 and j == 0
                            else cadd(starts[u][j], (zs[i, part * block + j, 0], zs[i, part * block + j, 1]))
                            for j in range(block)
                        ]
                    )
                for t in range(CHUNK):
                    power = [(table[i, t, 0], table[i, t, 1]) for i in ids]
                    for j in range(block):
                        at = pl.ds(aligned(((part * block + j) * CHUNK + t) * rows + h * HALF, HALF), HALF)
                        total = ys[at, :]
                        for u in range(pair):
                            total = total + (power[u][0] * states[u][j][0] - power[u][1] * states[u][j][1])
                        ys[at, :] = total

    enter(0)
    pl.semaphore_wait(barrier, row_len - 1 + n_rows - 1 + n_ch - 1)
    send_e(0)
    enter(1)
    send_e(1)
    enter(2)
    send_e(2)
    enter(3)
    send_e(3)
    send_t(0)
    near(0)
    send_t(1)
    near(1)
    prepare(0)
    send_s(0)
    send_t(2)
    prepare(1)
    prepare(2)
    send_s(1)
    send_t(3)
    prepare(3)
    send_s(2)
    far(0)
    send_s(3)
    far(1)
    far(2)
    far(3)

    q_load.wait()
    lane = lax.broadcasted_iota(jnp.int32, (16, LANES), 1)

    @pl.loop(0, tokens // 16)
    def _(g):
        toks = pl.ds(aligned(g * 16, 16), 16)
        squares = jnp.zeros((16, LANES), F32)
        for r in range(rows):
            lanes = pl.ds(r * LANES, LANES)
            at = pl.ds(g * (16 * rows) + r, 16, stride=rows)
            gated = q_buf[toks, lanes].astype(F32) * ys[at, :]
            gated_ref[pl.ds(aligned((g * rows + r) * 16, 16), 16), :] = gated
            squares = squares + gated * gated
        xs[toks, :] = squares

    power = jnp.zeros((16, LANES), F32)
    for g in range(tokens // 16):
        squares = xs[pl.ds(g * 16, 16), :]
        power = jnp.where(lane == g, jnp.sum(squares, axis=1, keepdims=True), power)
    p_all[my_ch] = power

    def remote_p(dst):
        return pltpu.make_async_remote_copy(
            src_ref=p_all.at[my_ch],
            dst_ref=p_all.at[my_ch],
            send_sem=p_send,
            recv_sem=p_recv,
            device_id={"ch": dst},
            device_id_type=MESH_IDS,
        )

    for step in range(1, n_ch):
        remote_p(lax.rem(my_ch + step, n_ch)).start()

    @pl.when(is_owner)
    def _():
        whole(e_stage, (OWNERS - 1) * halves * groups, e_send, e_recv.at[0]).wait_send()
        whole(s_out, (row_len - 1) * groups, s_send, s_recv.at[0, 0]).wait_send()
        for row in range(n_rows - 1):

            @pl.when(my_row == row)
            def _():
                whole(t_all, (n_rows - 1 - row) * groups, t_send, t_recv.at[0, 0]).wait_send()

    @pl.when(my_k >= OWNERS)
    def _():
        whole(e_stage, OWNERS * halves * groups, e_send, e_recv.at[0]).wait_send()

    @pl.when(me == 0)
    def _():
        for g in range(groups):
            for part in range(OWNERS // halves):
                wait_s(g, part)

    others = whole(p_all, n_ch - 1, p_send, p_recv)
    others.wait_recv()
    total = p_all[0]
    for c in range(1, n_ch):
        total = total + p_all[c]
    scale_ref[...] = lax.rsqrt(total * (1.0 / (rows * LANES * n_ch)) + EPS)
    others.wait_send()


def finish_kernel(gated_ref, scale_ref, gain_ref, out_hbm, out_buf, wide, sems):
    tokens, width = out_buf.shape
    rows = width // LANES
    parts = sems.shape[0]
    per_part = tokens // parts // 16
    for g in range(tokens // 16):
        wide[pl.ds(g * 16, 16), :] = jnp.broadcast_to(scale_ref[:, g : g + 1], (16, LANES))
    stores = []
    for n in range(parts):

        @pl.loop(n * per_part, (n + 1) * per_part)
        def _(g):
            toks = pl.ds(aligned(g * 16, 16), 16)
            scale = wide[toks, :]
            for r in range(rows):
                lanes = pl.ds(r * LANES, LANES)
                gated = gated_ref[pl.ds(aligned((g * rows + r) * 16, 16), 16), :]
                out_buf[toks, lanes] = (gated * gain_ref[:, lanes] * scale).astype(out_buf.dtype)

        toks = pl.ds(n * (tokens // parts), tokens // parts)
        stores.append(pltpu.make_async_copy(out_buf.at[toks], out_hbm.at[toks], sems.at[n]))
        stores[-1].start()
    for store in stores:
        store.wait()


def per_device(n_seq, n_ch, row_len, query, key, value, decay, angle, res_re, res_im, skip, gain):
    tokens, width = query.shape
    rows = width // LANES
    halves = rows // HALF
    slices = MODES * halves
    chunks = tokens // CHUNK
    n_rows = n_seq // row_len
    groups = MODES // OWNERS
    if groups != 4 or slices != groups * row_len or rows != 16 or chunks != 16 or halves != 2:
        raise ValueError("unsupported sizes")
    tile = (HALF, LANES)
    anywhere = pl.BlockSpec(memory_space=pl.ANY)
    vmem = pl.BlockSpec(memory_space=pltpu.VMEM)
    dma = pltpu.SemaphoreType.DMA
    operands = (query, key, value, decay, angle, res_re, res_im, skip.reshape(rows, LANES))
    gated, scale = pl.pallas_call(
        functools.partial(exchange_kernel, n_seq, n_ch, row_len),
        out_shape=(pltpu.VMEM((tokens * rows, LANES), F32), pltpu.VMEM((16, LANES), F32)),
        in_specs=[anywhere] * 8,
        out_specs=(vmem, vmem),
        scratch_shapes=[
            pltpu.VMEM((tokens, width), jnp.bfloat16),
            pltpu.VMEM((tokens, width), jnp.bfloat16),
            pltpu.VMEM((tokens, width), jnp.bfloat16),
            pltpu.VMEM((4, MODES, width), F32),
            pltpu.VMEM((rows, LANES), F32),
            pltpu.VMEM((tokens * rows, LANES), F32),
            pltpu.VMEM((tokens * rows, LANES), F32),
            pltpu.VMEM((6, MODES * rows, LANES), F32),
            pltpu.VMEM((CHUNK, halves) + tile, F32),
            pltpu.VMEM((slices, chunks, 2) + tile, F32),
            pltpu.VMEM((slices, CHUNK, 2) + tile, F32),
            pltpu.VMEM((slices, 4, 2) + tile, F32),
            pltpu.VMEM((slices, 2) + tile, F32),
            pltpu.VMEM((groups, row_len, halves, 2) + tile, F32),
            pltpu.VMEM((groups, halves, 2) + tile, F32),
            pltpu.VMEM((groups * n_rows, halves, 2) + tile, F32),
            pltpu.VMEM((groups * row_len, halves, 2) + tile, F32),
            pltpu.VMEM((2 * slices, 2) + tile, F32),
            pltpu.VMEM((n_ch, 16, LANES), F32),
            pltpu.VMEM((groups, halves, 2, 2) + tile, F32),
            dma((5,)),
            dma((2, 4)),
            dma(()),
            dma(()),
            dma((groups,)),
            dma(()),
            dma((groups, n_rows)),
            dma(()),
            dma((groups, OWNERS // halves)),
            dma(()),
            dma(()),
        ],
        compiler_params=pltpu.CompilerParams(collective_id=0, has_side_effects=True, vmem_limit_bytes=40 << 20),
    )(*(pltpu.with_memory_space_constraint(a, pltpu.HBM) for a in operands))
    gated = pltpu.with_memory_space_constraint(gated, pltpu.VMEM)
    scale = pltpu.with_memory_space_constraint(scale, pltpu.VMEM)
    return pl.pallas_call(
        finish_kernel,
        out_shape=jax.ShapeDtypeStruct((tokens, width), jnp.bfloat16),
        in_specs=[vmem, vmem, vmem],
        out_specs=anywhere,
        scratch_shapes=[pltpu.VMEM((tokens, width), jnp.bfloat16), pltpu.VMEM((tokens, LANES), F32), dma((4,))],
        compiler_params=pltpu.CompilerParams(vmem_limit_bytes=8 << 20),
    )(gated, scale, gain.reshape(1, width))


def solution(mesh):
    in_specs = (
        P("seq", "ch"),
        P("seq", "ch"),
        P("seq", "ch"),
        P(None, "ch"),
        P(None, "ch"),
        P(None, "ch"),
        P(None, "ch"),
        P("ch"),
        P("ch"),
    )
    return jax.shard_map(
        functools.partial(per_device, mesh.shape["seq"], mesh.shape["ch"], ROW_LEN),
        mesh=mesh,
        in_specs=in_specs,
        out_specs=P("seq", "ch"),
        check_vma=False,
    )
```

```python
import functools
import math

import jax
import jax.numpy as jnp
from jax import lax
from jax.experimental import pallas as pl
from jax.experimental.pallas import tpu as pltpu
from jax.sharding import PartitionSpec as P

F32 = jnp.float32
MODES = 16
CHUNK = 16
LANES = 128
HALF = 8
EPS = 1e-05
ROW_LEN = 8
OWNERS = 4
MESH_IDS = pl.DeviceIdType.MESH


def aligned(value, step):
    return pl.multiple_of(value, step)


def cmul(a, b):
    return a[0] * b[0] - a[1] * b[1], a[0] * b[1] + a[1] * b[0]


def csquare(a):
    cross = a[0] * a[1]
    return a[0] * a[0] - a[1] * a[1], cross + cross


def cadd(a, b):
    return a[0] + b[0], a[1] + b[1]


def sin_cos(angle):
    z = angle * 0.5
    w = z * z
    s = jnp.full_like(w, 1.0 / math.factorial(13))
    for n in (11, 9, 7, 5, 3, 1):
        s = s * w + ((-1.0) ** ((n - 1) // 2)) / math.factorial(n)
    s = s * z
    c = jnp.full_like(w, 1.0 / math.factorial(12))
    for n in (10, 8, 6, 4, 2, 0):
        c = c * w + ((-1.0) ** (n // 2)) / math.factorial(n)
    sc = s * c
    return sc + sc, 1.0 - 2.0 * (s * s)


def whole_power(decay, angle, count):
    v = angle * float(count)
    turns = jnp.floor(v * (0.5 / math.pi) + 0.5)
    first = 6.28125
    second = round((2.0 * math.pi - first) * 2.0**23) / 2.0**23
    third = 2.0 * math.pi - first - second
    rest = ((v - turns * first) - turns * second) - turns * third
    s, c = sin_cos(rest)
    magnitude = jnp.exp(decay * -float(count))
    return magnitude * c, magnitude * s


def exchange_kernel(
    n_seq,
    n_ch,
    row_len,
    q_hbm,
    k_hbm,
    v_hbm,
    decay_hbm,
    angle_hbm,
    res_re_hbm,
    res_im_hbm,
    skip_hbm,
    gated_ref,
    scale_ref,
    q_buf,
    k_buf,
    v_buf,
    raw,
    skip_buf,
    xs,
    ys,
    par,
    taps,
    zs,
    table,
    qpow,
    e_stage,
    e_row,
    t_out,
    t_all,
    s_out,
    s_all,
    p_all,
    jumps_ref,
    raw_sems,
    kv_sems,
    q_sem,
    e_send,
    e_recv,
    t_send,
    t_recv,
    s_send,
    s_recv,
    p_send,
    p_recv,
):
    me = lax.axis_index("seq")
    my_ch = lax.axis_index("ch")
    my_row = me // row_len
    my_k = lax.rem(me, row_len)
    n_rows = n_seq // row_len
    tokens = q_buf.shape[0]
    rows = q_buf.shape[1] // LANES
    chunks = tokens // CHUNK
    halves = rows // HALF
    slices = MODES * halves
    groups = MODES // OWNERS

    raw_loads = [
        pltpu.make_async_copy(src, raw.at[n], raw_sems.at[n])
        for n, src in enumerate((decay_hbm, angle_hbm, res_re_hbm, res_im_hbm))
    ]
    raw_loads.append(pltpu.make_async_copy(skip_hbm, skip_buf, raw_sems.at[4]))
    for load in raw_loads:
        load.start()
    parts = kv_sems.shape[1]
    kv_loads = []
    for n in range(parts):
        toks = pl.ds(n * (tokens // parts), tokens // parts)
        kv_loads.append(
            [
                pltpu.make_async_copy(k_hbm.at[toks], k_buf.at[toks], kv_sems.at[0, n]),
                pltpu.make_async_copy(v_hbm.at[toks], v_buf.at[toks], kv_sems.at[1, n]),
            ]
        )
        for load in kv_loads[-1]:
            load.start()
    q_load = pltpu.make_async_copy(q_hbm, q_buf, q_sem)

    def in_row(k):
        return {"seq": my_row * row_len + k}

    def other_k(step):
        return lax.rem(my_k + step, row_len)

    barrier = pltpu.get_barrier_semaphore()

    @pl.loop(1, row_len)
    def _(step):
        pl.semaphore_signal(barrier, inc=1, device_id=in_row(other_k(step)), device_id_type=MESH_IDS)

    @pl.loop(1, n_rows)
    def _(step):
        row = lax.rem(my_row + step, n_rows)
        pl.semaphore_signal(barrier, inc=1, device_id={"seq": row * row_len + my_k}, device_id_type=MESH_IDS)

    @pl.loop(1, n_ch)
    def _(step):
        pl.semaphore_signal(barrier, inc=1, device_id={"ch": lax.rem(my_ch + step, n_ch)}, device_id_type=MESH_IDS)

    for load in raw_loads:
        load.wait()

    @pl.loop(0, rows)
    def _(r):
        lanes = pl.ds(aligned(r * LANES, LANES), LANES)
        place = pl.ds(r, MODES, stride=rows)
        decay = raw[0, :, lanes]
        angle = raw[1, :, lanes]
        s, c = sin_cos(angle)
        magnitude = jnp.exp(-decay)
        weight = jnp.sqrt(decay)
        par[0, place, :] = magnitude * c
        par[1, place, :] = magnitude * s
        par[2, place, :] = weight * raw[2, :, lanes]
        par[3, place, :] = weight * raw[3, :, lanes]
        par[4, place, :] = decay
        par[5, place, :] = angle

    zero = jnp.zeros((HALF, LANES), F32)
    for h in range(halves):
        taps[0, h] = skip_buf[pl.ds(h * HALF, HALF), :]
        for n in range(1, CHUNK):
            taps[n, h] = zero

    @pl.when(me == 0)
    def _():
        @pl.loop(0, slices)
        def _(i):
            s_all[i, 0] = zero
            s_all[i, 1] = zero

    is_owner = my_k < OWNERS

    @pl.when(is_owner)
    def _():
        for g in range(groups):
            for h in range(halves):
                at = pl.ds(aligned((g * OWNERS + my_k) * rows + h * HALF, HALF), HALF)
                for n, count in enumerate((tokens, tokens * row_len)):
                    jump = whole_power(par[4, at, :], par[5, at, :], count)
                    jumps_ref[g, h, n, 0] = jump[0]
                    jumps_ref[g, h, n, 1] = jump[1]

    per_part = tokens // parts // 16
    for n in range(parts):
        for load in kv_loads[n]:
            load.wait()

        @pl.loop(n * per_part, (n + 1) * per_part)
        def _(g):
            toks = pl.ds(aligned(g * 16, 16), 16)
            for r in range(rows):
                lanes = pl.ds(r * LANES, LANES)
                xs[pl.ds(g * (16 * rows) + r, 16, stride=rows), :] = k_buf[toks, lanes].astype(F32) * v_buf[toks, lanes].astype(F32)

    q_load.start()

    def jumps(g, n):
        return [(jumps_ref[g, h, n, 0], jumps_ref[g, h, n, 1]) for h in range(halves)]

    def enter(g):
        @pl.loop(g * row_len, (g + 1) * row_len, unroll=2)
        def _(i):
            m = i // halves
            h = lax.rem(i, halves)
            here = pl.ds(aligned(m * rows + h * HALF, HALF), HALF)
            pole = (par[0, here, :], par[1, here, :])
            w = (par[2, here, :], par[3, here, :])
            z = [None] * chunks
            for n in range(CHUNK):
                taps[n, h] += w[0]
                for j in range(chunks):
                    x = xs[pl.ds(aligned((j * CHUNK + CHUNK - 1 - n) * rows + h * HALF, HALF), HALF), :]
                    term = (w[0] * x, w[1] * x)
                    z[j] = term if n == 0 else cadd(z[j], term)
                if n < CHUNK - 1:
                    w = cmul(w, pole)
            power = pole
            for _ in range(4):
                power = csquare(power)
            for j in range(chunks):
                zs[i, j, 0] = z[j][0]
                zs[i, j, 1] = z[j][1]
            level = 0
            while len(z) > 1:
                qpow[i, level, 0] = power[0]
                qpow[i, level, 1] = power[1]
                z = [cadd(cmul(z[2 * j], power), z[2 * j + 1]) for j in range(len(z) // 2)]
                level += 1
                if len(z) > 1:
                    power = csquare(power)
            e_stage[i, 0] = z[0][0]
            e_stage[i, 1] = z[0][1]

        @pl.when(is_owner)
        def _():
            for h in range(halves):
                e_row[g, my_k, h] = e_stage[(g * OWNERS + my_k) * halves + h]

    def mode_slices(g, k):
        return pl.ds((g * OWNERS + k) * halves, halves)

    def remote_e(g, k):
        return pltpu.make_async_remote_copy(
            src_ref=e_stage.at[mode_slices(g, k)],
            dst_ref=e_row.at[g, my_k],
            send_sem=e_send,
            recv_sem=e_recv.at[g],
            device_id=in_row(k),
            device_id_type=MESH_IDS,
        )

    def remote_t(g, row):
        return pltpu.make_async_remote_copy(
            src_ref=t_out.at[g],
            dst_ref=t_all.at[g * n_rows + my_row],
            send_sem=t_send,
            recv_sem=t_recv.at[g, my_row],
            device_id={"seq": row * row_len + my_k},
            device_id_type=MESH_IDS,
        )

    def remote_s(g, k):
        aside = (n_seq - (my_row * row_len + k)) // n_seq
        return pltpu.make_async_remote_copy(
            src_ref=s_out.at[g * row_len + k],
            dst_ref=s_all.at[pl.ds(aside * slices + (g * OWNERS + my_k) * halves, halves)],
            send_sem=s_send,
            recv_sem=s_recv.at[g, my_k // halves],
            device_id=in_row(k),
            device_id_type=MESH_IDS,
        )

    def whole(ref, count, send_sem, recv_sem):
        part = ref.at[pl.ds(0, count)]
        return pltpu.make_async_remote_copy(
            src_ref=part,
            dst_ref=part,
            send_sem=send_sem,
            recv_sem=recv_sem,
            device_id=in_row(other_k(1)),
            device_id_type=MESH_IDS,
        )

    def send_e(g):
        for k in range(OWNERS):

            @pl.when(k != my_k)
            def _():
                remote_e(g, k).start()

    def send_t(g):
        @pl.when(is_owner)
        def _():
            whole(e_row.at[g], row_len - 1, e_send, e_recv.at[g]).wait_recv()
            jump = jumps(g, 0)
            for h in range(halves):
                total = (e_row[g, 0, h, 0], e_row[g, 0, h, 1])
                for k in range(1, row_len):
                    total = cadd(cmul(total, jump[h]), (e_row[g, k, h, 0], e_row[g, k, h, 1]))
                t_out[g, h, 0] = total[0]
                t_out[g, h, 1] = total[1]
            for row in range(1, n_rows):

                @pl.when(my_row < row)
                def _():
                    remote_t(g, row).start()

    def send_s(g):
        @pl.when(is_owner)
        def _():
            jump, row_jump = jumps(g, 0), jumps(g, 1)

            def add_row(row, states):
                pltpu.make_async_remote_copy(
                    src_ref=t_out.at[g],
                    dst_ref=t_all.at[g * n_rows + row],
                    send_sem=t_send,
                    recv_sem=t_recv.at[g, row],
                    device_id=in_row(other_k(1)),
                    device_id_type=MESH_IDS,
                ).wait_recv()
                at = g * n_rows + row
                return tuple(
                    cadd(cmul(states[h], row_jump[h]), (t_all[at, h, 0], t_all[at, h, 1])) for h in range(halves)
                )

            states = lax.fori_loop(0, my_row, add_row, ((zero, zero),) * halves)
            for h in range(halves):
                state = states[h]
                for k in range(row_len):
                    s_out[g * row_len + k, h, 0] = state[0]
                    s_out[g * row_len + k, h, 1] = state[1]
                    if k < row_len - 1:
                        state = cadd(cmul(state, jump[h]), (e_row[g, k, h, 0], e_row[g, k, h, 1]))
            for h in range(halves):
                s_all[(g * OWNERS + my_k) * halves + h] = s_out[g * row_len + my_k, h]
            for step in range(1, row_len):
                remote_s(g, other_k(step)).start()

    def wait_s(g, part):
        @pl.when(my_k // halves == part)
        def _():
            whole(s_all, halves, s_send, s_recv.at[g, part]).wait_recv()

        @pl.when(my_k // halves != part)
        def _():
            whole(s_all, halves * halves, s_send, s_recv.at[g, part]).wait_recv()

    def near(h):
        @pl.loop(0, chunks, unroll=4)
        def _(j):
            tap = [taps[n, h] for n in range(CHUNK)]
            x = [xs[pl.ds(aligned((j * CHUNK + s) * rows + h * HALF, HALF), HALF), :] for s in range(CHUNK)]
            for t in range(CHUNK):
                total = tap[t] * x[0]
                for s in range(1, t + 1):
                    total = total + tap[t - s] * x[s]
                ys[pl.ds(aligned((j * CHUNK + t) * rows + h * HALF, HALF), HALF), :] = total

    def prepare(g):
        unit = 4

        @pl.loop(0, row_len // unit)
        def _(b):
            ids = [g * row_len + b * unit + u for u in range(unit)]
            step = [(qpow[i, 0, 0], qpow[i, 0, 1]) for i in ids]
            states = [(zs[i, 0, 0], zs[i, 0, 1]) for i in ids]
            poles = []
            for i in ids:
                here = pl.ds(aligned((i // halves) * rows + lax.rem(i, halves) * HALF, HALF), HALF)
                poles.append((par[0, here, :], par[1, here, :]))
            powers = list(poles)
            for j in range(1, chunks):
                for u, i in enumerate(ids):
                    if j < chunks - 1:
                        following = cadd(cmul(states[u], step[u]), (zs[i, j, 0], zs[i, j, 1]))
                    zs[i, j, 0] = states[u][0]
                    zs[i, j, 1] = states[u][1]
                    if j < chunks - 1:
                        states[u] = following
            for t in range(CHUNK):
                for u, i in enumerate(ids):
                    table[i, t, 0] = powers[u][0]
                    table[i, t, 1] = powers[u][1]
                    if t < CHUNK - 1:
                        powers[u] = cmul(powers[u], poles[u])

    pair = 2
    block = chunks // 2

    def far(g):
        @pl.loop(0, row_len // pair)
        def _(b):
            @pl.when((me > 0) & (lax.rem(b, halves) == 0))
            def _():
                wait_s(g, b // halves)

            h = lax.rem(b, halves)
            first = g * row_len + (b // halves) * (pair * halves) + h
            ids = [first + u * halves for u in range(pair)]
            starts = []
            for i in ids:
                d = [(s_all[i, 0], s_all[i, 1])]
                for level in range(3):
                    power = (qpow[i, level, 0], qpow[i, level, 1])
                    d = d + [cmul(a, power) for a in d]
                starts.append(d)
            for part in range(2):
                states = []
                for u, i in enumerate(ids):
                    if part == 1:
                        power = (qpow[i, 3, 0], qpow[i, 3, 1])
                        starts[u] = [cmul(a, power) for a in starts[u]]
                    states.append(
                        [
                            starts[u][j]
                            if part == 0 and j == 0
                            else cadd(starts[u][j], (zs[i, part * block + j, 0], zs[i, part * block + j, 1]))
                            for j in range(block)
                        ]
                    )
                for t in range(CHUNK):
                    power = [(table[i, t, 0], table[i, t, 1]) for i in ids]
                    for j in range(block):
                        at = pl.ds(aligned(((part * block + j) * CHUNK + t) * rows + h * HALF, HALF), HALF)
                        total = ys[at, :]
                        for u in range(pair):
                            total = total + (power[u][0] * states[u][j][0] - power[u][1] * states[u][j][1])
                        ys[at, :] = total

    enter(0)
    pl.semaphore_wait(barrier, row_len - 1 + n_rows - 1 + n_ch - 1)
    send_e(0)
    enter(1)
    send_e(1)
    enter(2)
    send_e(2)
    enter(3)
    send_e(3)
    send_t(0)
    near(0)
    send_t(1)
    near(1)
    prepare(0)
    send_s(0)
    send_t(2)
    prepare(1)
    prepare(2)
    send_s(1)
    send_t(3)
    prepare(3)
    send_s(2)
    far(0)
    send_s(3)
    far(1)
    far(2)
    far(3)

    q_load.wait()
    lane = lax.broadcasted_iota(jnp.int32, (16, LANES), 1)

    @pl.loop(0, tokens // 16)
    def _(g):
        toks = pl.ds(aligned(g * 16, 16), 16)
        squares = jnp.zeros((16, LANES), F32)
        for r in range(rows):
            lanes = pl.ds(r * LANES, LANES)
            at = pl.ds(g * (16 * rows) + r, 16, stride=rows)
            gated = q_buf[toks, lanes].astype(F32) * ys[at, :]
            gated_ref[pl.ds(aligned((g * rows + r) * 16, 16), 16), :] = gated
            squares = squares + gated * gated
        xs[toks, :] = squares

    power = jnp.zeros((16, LANES), F32)
    for g in range(tokens // 16):
        squares = xs[pl.ds(g * 16, 16), :]
        power = jnp.where(lane == g, jnp.sum(squares, axis=1, keepdims=True), power)
    p_all[my_ch] = power

    def remote_p(dst):
        return pltpu.make_async_remote_copy(
            src_ref=p_all.at[my_ch],
            dst_ref=p_all.at[my_ch],
            send_sem=p_send,
            recv_sem=p_recv,
            device_id={"ch": dst},
            device_id_type=MESH_IDS,
        )

    for step in range(1, n_ch):
        remote_p(lax.rem(my_ch + step, n_ch)).start()

    @pl.when(is_owner)
    def _():
        whole(e_stage, (OWNERS - 1) * halves * groups, e_send, e_recv.at[0]).wait_send()
        whole(s_out, (row_len - 1) * groups, s_send, s_recv.at[0, 0]).wait_send()
        for row in range(n_rows - 1):

            @pl.when(my_row == row)
            def _():
                whole(t_all, (n_rows - 1 - row) * groups, t_send, t_recv.at[0, 0]).wait_send()

    @pl.when(my_k >= OWNERS)
    def _():
        whole(e_stage, OWNERS * halves * groups, e_send, e_recv.at[0]).wait_send()

    @pl.when(me == 0)
    def _():
        for g in range(groups):
            for part in range(OWNERS // halves):
                wait_s(g, part)

    others = whole(p_all, n_ch - 1, p_send, p_recv)
    others.wait_recv()
    total = p_all[0]
    for c in range(1, n_ch):
        total = total + p_all[c]
    scale_ref[...] = lax.rsqrt(total * (1.0 / (rows * LANES * n_ch)) + EPS)
    others.wait_send()


def finish_kernel(gated_ref, scale_ref, gain_ref, out_hbm, out_buf, wide, sems):
    tokens, width = out_buf.shape
    rows = width // LANES
    parts = sems.shape[0]
    per_part = tokens // parts // 16
    for g in range(tokens // 16):
        wide[pl.ds(g * 16, 16), :] = jnp.broadcast_to(scale_ref[:, g : g + 1], (16, LANES))
    stores = []
    for n in range(parts):

        @pl.loop(n * per_part, (n + 1) * per_part)
        def _(g):
            toks = pl.ds(aligned(g * 16, 16), 16)
            scale = wide[toks, :]
            for r in range(rows):
                lanes = pl.ds(r * LANES, LANES)
                gated = gated_ref[pl.ds(aligned((g * rows + r) * 16, 16), 16), :]
                out_buf[toks, lanes] = (gated * gain_ref[:, lanes] * scale).astype(out_buf.dtype)

        toks = pl.ds(n * (tokens // parts), tokens // parts)
        stores.append(pltpu.make_async_copy(out_buf.at[toks], out_hbm.at[toks], sems.at[n]))
        stores[-1].start()
    for store in stores:
        store.wait()


def per_device(n_seq, n_ch, row_len, query, key, value, decay, angle, res_re, res_im, skip, gain):
    tokens, width = query.shape
    rows = width // LANES
    halves = rows // HALF
    slices = MODES * halves
    chunks = tokens // CHUNK
    n_rows = n_seq // row_len
    groups = MODES // OWNERS
    if groups != 4 or slices != groups * row_len or rows != 16 or chunks != 16 or halves != 2:
        raise ValueError("unsupported sizes")
    tile = (HALF, LANES)
    anywhere = pl.BlockSpec(memory_space=pl.ANY)
    vmem = pl.BlockSpec(memory_space=pltpu.VMEM)
    dma = pltpu.SemaphoreType.DMA
    operands = (query, key, value, decay, angle, res_re, res_im, skip.reshape(rows, LANES))
    gated, scale = pl.pallas_call(
        functools.partial(exchange_kernel, n_seq, n_ch, row_len),
        out_shape=(pltpu.VMEM((tokens * rows, LANES), F32), pltpu.VMEM((16, LANES), F32)),
        in_specs=[anywhere] * 8,
        out_specs=(vmem, vmem),
        scratch_shapes=[
            pltpu.VMEM((tokens, width), jnp.bfloat16),
            pltpu.VMEM((tokens, width), jnp.bfloat16),
            pltpu.VMEM((tokens, width), jnp.bfloat16),
            pltpu.VMEM((4, MODES, width), F32),
            pltpu.VMEM((rows, LANES), F32),
            pltpu.VMEM((tokens * rows, LANES), F32),
            pltpu.VMEM((tokens * rows, LANES), F32),
            pltpu.VMEM((6, MODES * rows, LANES), F32),
            pltpu.VMEM((CHUNK, halves) + tile, F32),
            pltpu.VMEM((slices, chunks, 2) + tile, F32),
            pltpu.VMEM((slices, CHUNK, 2) + tile, F32),
            pltpu.VMEM((slices, 4, 2) + tile, F32),
            pltpu.VMEM((slices, 2) + tile, F32),
            pltpu.VMEM((groups, row_len, halves, 2) + tile, F32),
            pltpu.VMEM((groups, halves, 2) + tile, F32),
            pltpu.VMEM((groups * n_rows, halves, 2) + tile, F32),
            pltpu.VMEM((groups * row_len, halves, 2) + tile, F32),
            pltpu.VMEM((2 * slices, 2) + tile, F32),
            pltpu.VMEM((n_ch, 16, LANES), F32),
            pltpu.VMEM((groups, halves, 2, 2) + tile, F32),
            dma((5,)),
            dma((2, 4)),
            dma(()),
            dma(()),
            dma((groups,)),
            dma(()),
            dma((groups, n_rows)),
            dma(()),
            dma((groups, OWNERS // halves)),
            dma(()),
            dma(()),
        ],
        compiler_params=pltpu.CompilerParams(collective_id=0, has_side_effects=True, vmem_limit_bytes=40 << 20),
    )(*(pltpu.with_memory_space_constraint(a, pltpu.HBM) for a in operands))
    gated = pltpu.with_memory_space_constraint(gated, pltpu.VMEM)
    scale = pltpu.with_memory_space_constraint(scale, pltpu.VMEM)
    return pl.pallas_call(
        finish_kernel,
        out_shape=jax.ShapeDtypeStruct((tokens, width), jnp.bfloat16),
        in_specs=[vmem, vmem, vmem],
        out_specs=anywhere,
        scratch_shapes=[pltpu.VMEM((tokens, width), jnp.bfloat16), pltpu.VMEM((tokens, LANES), F32), dma((4,))],
        compiler_params=pltpu.CompilerParams(vmem_limit_bytes=8 << 20),
    )(gated, scale, gain.reshape(1, width))


def solution(mesh):
    in_specs = (
        P("seq", "ch"),
        P("seq", "ch"),
        P("seq", "ch"),
        P(None, "ch"),
        P(None, "ch"),
        P(None, "ch"),
        P(None, "ch"),
        P("ch"),
        P("ch"),
    )
    return jax.shard_map(
        functools.partial(per_device, mesh.shape["seq"], mesh.shape["ch"], ROW_LEN),
        mesh=mesh,
        in_specs=in_specs,
        out_specs=P("seq", "ch"),
        check_vma=False,
    )
```
